512 devices in a mesh: gx: 32 (over x, y, core), gy: 16 (over z).
Axes of the slice: x: 4, y: 4, z: 16, core: 2. Of those that a mesh axis runs over, the one named last changes fastest.
Arguments:
- momenta: float32 [3, 16, 128, 4096], P(None, None, 'gy', 'gx'), may hold values from -6 to 6
- theta: float32 [16, 128, 4096], P(None, 'gy', 'gx'), may hold values from -6 to 6
- courant: float32 [3, 16, 128, 4096], P(None, None, 'gy', 'gx'), may hold values from -0.3 to 0.3
- density: float32 [16, 128, 4096], P(None, 'gy', 'gx'), may hold values from 0.8 to 1.6
- metric_diag: float32 [3, 16, 128, 4096], P(None, None, 'gy', 'gx'), may hold values from 0.5 to 2
- metric_cross: float32 [3, 16, 128, 4096], P(None, None, 'gy', 'gx'), may hold values from -0.2 to 0.2
Outputs:
- momenta_out: float32 [3, 16, 128, 4096], P(None, None, 'gy', 'gx')
- theta_out: float32 [16, 128, 4096], P(None, 'gy', 'gx')
- pressure: float32 [16, 128, 4096], P(None, 'gy', 'gx')
The draws below stay inside these ranges and needn't reach their ends.
All inputs are finite; a program needn't handle non-finite values.
Results may differ from the reference program's by a relative error of at most 0.0003.
Values sent between devices are 32-bit elements; how exact they have to be, the bound alone decides.
No kernel may reach another device: no remote copies, remote signals or barrier semaphores. Data moves between devices by JAX's collectives and lax.ppermute only.
A program may use at most 64 MiB of HBM per device.

```python
import math
import jax
import jax.numpy as jnp

NZ = 16
ITERS = 3
NX = 4096
NY = 128


def steps_of(key, shape, pieces, low, top_value):
    def one(axis_at, shards_of):
        draws = jax.random.uniform(jax.random.fold_in(jax.random.fold_in(key, 6), axis_at), (shards_of,), jnp.float32, low / len(pieces), top_value / len(pieces))
        return jnp.repeat(jnp.exp(draws), shape[axis_at] // shards_of).reshape((-1,) + (1,) * (len(shape) - axis_at - 1))

    factor_of = one(*pieces[0])
    for cut in pieces[1:]:
        factor_of = factor_of * one(*cut)
    return factor_of


def centred(stream_key, dims, width, bound, cuts=(), held_as=jnp.bfloat16):
    values = jax.random.normal(stream_key, dims, jnp.float32) * width
    if len(cuts) > 0:
        values = steps_of(stream_key, dims, cuts, -0.22, 0.18) * values
    return jnp.clip(values, min=-bound, max=bound).astype(held_as)


def setup_inputs(seed: int = 0) -> dict:
    key_of = jax.random.split(jax.random.key(seed), 7)
    momenta = centred(key_of[0], (3, NZ, NY, NX), 1.0, 6.0, ((2, 16), (3, 32)), jnp.float32)
    theta = centred(key_of[1], (NZ, NY, NX), 1.0, 6.0, ((1, 16), (2, 32)), jnp.float32)
    courant = jnp.clip(jax.random.uniform(key_of[2], (3, NZ, NY, NX), jnp.float32, -0.3, 0.3) * steps_of(key_of[2], (3, NZ, NY, NX), ((2, 16), (3, 32)), -0.4, 0.0), -0.3, 0.3)
    density = jnp.clip(0.8 + 0.8 * jax.random.uniform(key_of[3], (NZ, NY, NX), jnp.float32) ** steps_of(key_of[3], (NZ, NY, NX), ((1, 16), (2, 32)), -0.2, 0.2), 0.8, 1.6)
    metric_diag = jnp.clip(jnp.exp(math.log(2.0) - 1.3862944 * jax.random.uniform(key_of[4], (3, NZ, NY, NX), jnp.float32) ** steps_of(key_of[4], (3, NZ, NY, NX), ((2, 16), (3, 32)), -0.2, 0.2)), 0.5, 2.0)
    metric_cross = jnp.clip(jax.random.uniform(key_of[5], (3, NZ, NY, NX), jnp.float32, -0.2, 0.2) * steps_of(key_of[5], (3, NZ, NY, NX), ((2, 16), (3, 32)), -0.4, 0.0), -0.2, 0.2)
    return {"momenta": momenta, "theta": theta, "courant": courant, "density": density, "metric_diag": metric_diag, "metric_cross": metric_cross}


helm = 0.02


def zshift(a, dz):
    if dz == 0:
        return a
    if dz > 0:
        return jnp.concatenate((a[..., dz:, :, :], jnp.zeros_like(a[..., :dz, :, :])), axis=-3)
    return jnp.concatenate((jnp.zeros_like(a[..., dz:, :, :]), a[..., :dz, :, :]), axis=-3)


def yshift(a, dy):
    if dy == 0:
        return a
    if dy > 0:
        return jnp.concatenate((a[..., dy:, :], jnp.zeros_like(a[..., :dy, :])), axis=-2)
    return jnp.concatenate((jnp.zeros_like(a[..., dy:, :]), a[..., :dy, :]), axis=-2)


def shifted(a, dz, dy, dx):
    if dx != 0:
        a = jnp.roll(a, -dx, axis=-1)
    return zshift(yshift(a, dy), dz)


def donor(left, right, courant):
    return jnp.maximum(courant, 0.0) * left + jnp.minimum(courant, 0.0) * right


def antidiff(left, right, courant, dens_left, dens_right):
    return 0.5 * (jnp.abs(courant) - courant * courant / (0.5 * (dens_left + dens_right))) * (right - left)


def upwind_pass(look, field, dens, cx, cy, cz):
    centre = look(field, 0, 0, 0)
    fxr = donor(centre, look(field, 0, 0, 1), look(cx, 0, 0, 1))
    fxl = donor(look(field, 0, 0, -1), centre, look(cx, 0, 0, 0))
    fyr = donor(centre, look(field, 0, 1, 0), look(cy, 0, 1, 0))
    fyl = donor(look(field, 0, -1, 0), centre, look(cy, 0, 0, 0))
    fzr = donor(centre, look(field, 1, 0, 0), look(cz, 1, 0, 0))
    fzl = donor(look(field, -1, 0, 0), centre, look(cz, 0, 0, 0))
    return centre - (fxr - fxl + fyr - fyl + fzr - fzl) / look(dens, 0, 0, 0)


def anti_pass(look_new, look_old, first, dens, cx, cy, cz):
    centre = look_new(first, 0, 0, 0)
    here = look_old(dens, 0, 0, 0)
    axr = antidiff(centre, look_new(first, 0, 0, 1), look_old(cx, 0, 0, 1), here, look_old(dens, 0, 0, 1))
    axl = antidiff(look_new(first, 0, 0, -1), centre, look_old(cx, 0, 0, 0), look_old(dens, 0, 0, -1), here)
    ayr = antidiff(centre, look_new(first, 0, 1, 0), look_old(cy, 0, 1, 0), here, look_old(dens, 0, 1, 0))
    ayl = antidiff(look_new(first, 0, -1, 0), centre, look_old(cy, 0, 0, 0), look_old(dens, 0, -1, 0), here)
    azr = antidiff(centre, look_new(first, 1, 0, 0), look_old(cz, 1, 0, 0), here, look_old(dens, 1, 0, 0))
    azl = antidiff(look_new(first, -1, 0, 0), centre, look_old(cz, 0, 0, 0), look_old(dens, -1, 0, 0), here)
    return centre - (axr - axl + ayr - ayl + azr - azl) / here


def coefficients(look, a_one, a_two, a_three, cross, upper_y, lower_y, upper_z, lower_z):
    wx = 0.5 * (look(a_one, 0, 0, 0) + look(a_one, 0, 0, 1))
    wxl = 0.5 * (look(a_one, 0, 0, -1) + look(a_one, 0, 0, 0))
    wy = 0.5 * (look(a_two, 0, 0, 0) + look(a_two, 0, 1, 0)) * upper_y
    wyl = 0.5 * (look(a_two, 0, -1, 0) + look(a_two, 0, 0, 0)) * lower_y
    wz = 0.5 * (a_three + zshift(a_three, 1)) * upper_z
    wzl = 0.5 * (zshift(a_three, -1) + a_three) * lower_z
    return (wx, wxl, wy, wyl, wz, wzl, cross[0], cross[1], cross[2])


def operate(look, field, coef):
    wx, wxl, wy, wyl, wz, wzl, c_xy, c_xz, c_yz = coef
    centre = look(field, 0, 0, 0)
    flow_x = wx * (look(field, 0, 0, 1) - centre) - wxl * (centre - look(field, 0, 0, -1))
    flow_y = wy * (look(field, 0, 1, 0) - centre) - wyl * (centre - look(field, 0, -1, 0))
    flow_z = wz * (look(field, 1, 0, 0) - centre) - wzl * (centre - look(field, -1, 0, 0))
    d_xy = 0.25 * ((look(field, 0, 1, 1) - look(field, 0, 1, -1)) - (look(field, 0, -1, 1) - look(field, 0, -1, -1)))
    d_xz = 0.25 * ((look(field, 1, 0, 1) - look(field, 1, 0, -1)) - (look(field, -1, 0, 1) - look(field, -1, 0, -1)))
    d_yz = 0.25 * ((look(field, 1, 1, 0) - look(field, 1, -1, 0)) - (look(field, -1, 1, 0) - look(field, -1, -1, 0)))
    return flow_x + flow_y + flow_z + c_xy * d_xy + c_xz * d_xz + c_yz * d_yz - helm * centre


def reference(momenta, theta, courant, density, metric_diag, metric_cross):
    rows = jnp.arange(NY, dtype=jnp.int32)[:, None]
    levels = jnp.arange(NZ, dtype=jnp.int32)[:, None, None]
    cx = courant[0]
    cy = courant[1] * (rows != 0).astype(jnp.float32)
    cz = courant[2] * (levels != 0).astype(jnp.float32)
    fields = [momenta[0], momenta[1], momenta[2], theta]
    moved = []
    for field in fields:
        first = upwind_pass(shifted, field, density, cx, cy, cz)
        moved.append(anti_pass(shifted, shifted, first, density, cx, cy, cz))
    uflow, vflow, wflow, theta_out = moved
    rhs = 0.5 * (shifted(uflow, 0, 0, 1) - shifted(uflow, 0, 0, -1)) + 0.5 * (shifted(vflow, 0, 1, 0) - shifted(vflow, 0, -1, 0)) + 0.5 * (zshift(wflow, 1) - zshift(wflow, -1))
    upper_y = (rows < NY - 1).astype(jnp.float32)
    lower_y = (rows > 0).astype(jnp.float32)
    upper_z = (levels < NZ - 1).astype(jnp.float32)
    lower_z = (levels > 0).astype(jnp.float32)
    coef = coefficients(shifted, metric_diag[0], metric_diag[1], metric_diag[2], metric_cross, upper_y, lower_y, upper_z, lower_z)
    solution = jnp.zeros_like(rhs)
    resid = rhs
    dirs = [resid]
    images = [operate(shifted, resid, coef)]
    norms = [jnp.sum(images[0] * images[0])]
    for step in range(ITERS):
        beta = jnp.sum(resid * images[step]) / norms[step]
        solution = solution + beta * dirs[step]
        resid = resid - beta * images[step]
        if step + 1 < ITERS:
            lifted = operate(shifted, resid, coef)
            new_dir = resid
            new_img = lifted
            for back in range(step + 1):
                alpha = jnp.sum(lifted * images[back]) / norms[back]
                new_dir = new_dir - alpha * dirs[back]
                new_img = new_img - alpha * images[back]
            dirs.append(new_dir)
            images.append(new_img)
            norms.append(jnp.sum(new_img * new_img))
    grad_x = 0.5 * (shifted(solution, 0, 0, 1) - shifted(solution, 0, 0, -1))
    grad_y = 0.5 * (shifted(solution, 0, 1, 0) - shifted(solution, 0, -1, 0))
    grad_z = 0.5 * (zshift(solution, 1) - zshift(solution, -1))
    momenta_out = jnp.stack((uflow - grad_x, vflow - grad_y, wflow - grad_z), axis=0)
    return momenta_out, theta_out, solution
```

```python
import jax
import jax.numpy as jnp
from jax import lax
from jax.experimental import pallas as pl
from jax.experimental.pallas import tpu as pltpu
from jax.sharding import PartitionSpec as P

helm = 0.02
ITERS = 3
NF = 14
U, V, W, TH, G, CX, CY, CZ, A11, A22, A33, A12, A13, A23 = range(NF)
COMBOS = (
    (V, 6, TH, 2),
    (CY, 6, A12, 2),
    (U, 5, A22, 3),
    (W, 5, A11, 2),
    (G, 5, A33, 2),
    (CX, 5, A13, 2),
    (CZ, 5, A23, 2),
)
F32 = jnp.float32


def lanes(shape):
    return lax.broadcasted_iota(jnp.int32, shape, len(shape) - 1)


def rows(shape):
    return lax.broadcasted_iota(jnp.int32, shape, len(shape) - 2)


def roll(a, shift, axis):
    shift = shift % a.shape[axis]
    if shift == 0:
        return a
    return pltpu.roll(a, shift, axis)


def xs(a, d):
    return roll(a, -d, 1)


def ys(a, d):
    return roll(a, -d, 0)


def field_of(refs, f):
    mom, th, cou, den, dia, cro = refs
    if f < 3:
        return mom.at[f]
    if f == TH:
        return th
    if f == G:
        return den
    if f < 8:
        return cou.at[f - 5]
    if f < 11:
        return dia.at[f - 8]
    return cro.at[f - 11]


def pack_kernel(mom, th, cou, den, dia, cro, to_left, to_right, to_up, to_down):
    refs = (mom, th, cou, den, dia, cro)
    nz = den.shape[0]
    lane = lanes((8, 128)) // 8
    row = rows((8, 128))
    for f in range(NF):
        ref = field_of(refs, f)
        left = jnp.zeros((8, 128), F32)
        right = jnp.zeros((8, 128), F32)
        for k in range(nz):
            moved = roll(ref[k], 8 * k, 1)
            left = jnp.where(lane == k, moved, left)
            right = jnp.where(lane == (k - 1) % nz, moved, right)
        to_left[f] = left
        to_right[f] = right
    for c, (first, n, second, m) in enumerate(COMBOS):
        one, two = field_of(refs, first), field_of(refs, second)
        for k in range(nz):
            a, b = one[k], two[k]
            to_down[c, k] = jnp.where(row < n, a, roll(b, n, 0))
            to_up[c, k] = jnp.where(row >= 8 - n, a, roll(b, -n, 0))


def main_kernel(
    mom, th, cou, den, dia, cro, from_left, from_right, below, above, cbelow, cabove,
    moved, theta_out, basis, dxs, dys, gram,
    S, P1, M, IG, C, VV, D, E, T,
):
    refs = (mom, th, cou, den, dia, cro)
    nz = den.shape[0]
    gy = lax.axis_index("gy")
    ny = lax.axis_size("gy")
    has_below = gy > 0
    has_above = gy < ny - 1
    shape = (24, 256)
    lane128 = lanes((8, 128))
    row24 = rows(shape)
    inside = ((row24 >= 8) | has_below) & ((row24 < 16) | has_above)
    edge_row = ((row24 == 8) & ~has_below) | ((row24 == 16) & ~has_above)

    for c, (first, n, second, m) in enumerate(COMBOS):
        for f, shift in ((first, 0), (second, n)):
            ref = field_of(refs, f)
            outside = 1.0 if f == G else 0.0

            def rows_in(k, carry, f=f, shift=shift, c=c, ref=ref, outside=outside):
                low = roll(below[c, k], shift, 0)
                high = roll(above[c, k], -shift, 0)
                S[f, k + 1, 0:8, 0:128] = jnp.where(has_below, low, outside)
                S[f, k + 1, 8:16, 0:128] = ref[k]
                S[f, k + 1, 16:24, 0:128] = jnp.where(has_above, high, outside)
                return carry

            lax.fori_loop(0, nz, rows_in, 0, unroll=True)
    for f in range(NF):
        outside = 1.0 if f == G else 0.0
        for g, (left, right) in enumerate(
            (
                (cbelow[f], cbelow[NF + f]),
                (from_left[f], from_right[f]),
                (cabove[f], cabove[NF + f]),
            )
        ):
            if g == 0:
                left, right = (jnp.where(has_below, a, outside) for a in (left, right))
            if g == 2:
                left, right = (jnp.where(has_above, a, outside) for a in (left, right))
            for k in range(nz):
                S[f, k + 1, 8 * g : 8 * g + 8, 128:256] = jnp.where(
                    lane128 < 64, roll(right, -8 * k, 1), roll(left, -8 * k, 1)
                )
        pad = jnp.full(shape, outside, F32)
        S[f, 0] = pad
        S[f, nz + 1] = pad
    zero = jnp.zeros(shape, F32)
    S[CZ, 1] = zero

    def upwind(k, fz):
        cx, cy, cz = S[CX, k], S[CY, k], S[CZ, k + 1]
        cy = jnp.where(edge_row, 0.0, cy)
        S[CY, k] = cy
        ig = 1.0 / S[G, k]
        IG[k] = ig
        xp, xm = jnp.maximum(cx, 0.0), jnp.minimum(cx, 0.0)
        yp, ym = jnp.maximum(cy, 0.0), jnp.minimum(cy, 0.0)
        zp, zm = jnp.maximum(cz, 0.0), jnp.minimum(cz, 0.0)
        out = []
        for f in range(4):
            psi = S[f, k]
            fx = xp * xs(psi, -1) + xm * psi
            fy = yp * ys(psi, -1) + ym * psi
            up = zp * psi + zm * S[f, k + 1]
            P1[f, k] = psi - (xs(fx, 1) - fx + ys(fy, 1) - fy + up - fz[f]) * ig
            out.append(up)
        return tuple(out)

    lax.fori_loop(1, nz + 1, upwind, (zero,) * 4)
    for f in range(4):
        P1[f, 0] = zero
        P1[f, nz + 1] = zero

    def face(c, one, two):
        return 0.5 * (jnp.abs(c) - c * c / (0.5 * (one + two)))

    def anti(k, az):
        dens = S[G, k]
        kx = face(S[CX, k], xs(dens, -1), dens)
        ky = face(S[CY, k], ys(dens, -1), dens)
        kz = face(S[CZ, k + 1], dens, S[G, k + 1])
        ig = IG[k]
        out = []
        for f in range(4):
            psi = P1[f, k]
            ax = kx * (psi - xs(psi, -1))
            ay = ky * (psi - ys(psi, -1))
            up = kz * (P1[f, k + 1] - psi)
            res = psi - (xs(ax, 1) - ax + ys(ay, 1) - ay + up - az[f]) * ig
            if f < 3:
                M[f, k] = res
                moved[f, k - 1] = res[8:16, 0:128]
            else:
                theta_out[k - 1] = res[8:16, 0:128]
            out.append(up)
        return tuple(out)

    lax.fori_loop(1, nz + 1, anti, (zero,) * 4)
    M[2, 0] = zero
    M[2, nz + 1] = zero

    def first(k, carry):
        u, v = M[0, k], M[1, k]
        rhs = 0.5 * (
            (xs(u, 1) - xs(u, -1)) + (ys(v, 1) - ys(v, -1)) + (M[2, k + 1] - M[2, k - 1])
        )
        VV[0, k] = jnp.where(inside, rhs, 0.0)
        a11, a22, a33 = S[A11, k], S[A22, k], S[A33, k]
        wxl = 0.5 * (xs(a11, -1) + a11)
        wyl = jnp.where(edge_row, 0.0, 0.5 * (ys(a22, -1) + a22))
        wzl = jnp.where(k > 1, 0.5 * (S[A33, k - 1] + a33), 0.0)
        wz = jnp.where(k < nz, 0.5 * (S[A33, k + 1] + a33), 0.0)
        wx, wy = xs(wxl, 1), ys(wyl, 1)
        C[0, k] = wx
        C[1, k] = wxl
        C[2, k] = wy
        C[3, k] = wyl
        C[4, k] = wz
        C[5, k] = wzl
        C[6, k] = ((wx + wxl) + (wy + wyl)) + ((wz + wzl) + helm)
        C[7, k] = 0.25 * S[A12, k]
        C[8, k] = 0.25 * S[A13, k]
        C[9, k] = 0.25 * S[A23, k]
        return carry

    lax.fori_loop(1, nz + 1, first, 0)
    for i in range(3):
        VV[i, 0] = zero
        VV[i, nz + 1] = zero
    for a in (D, E):
        a[0] = zero
        a[nz + 1] = zero

    own = lambda a: a[8:16, 0:128]
    sums = {}
    for i in range(3):
        last = i == 2
        cut = own if last else (lambda a: a)

        def flat(k, carry, i=i, cut=cut):
            p = VV[i, k]
            xp, xm, yp, ym = xs(p, 1), xs(p, -1), ys(p, 1), ys(p, -1)
            d, e = xp - xm, yp - ym
            D[k] = d
            E[k] = e
            dxs[i, k - 1] = own(d)
            dys[i, k - 1] = own(e)
            basis[i, k - 1] = own(p)
            dxy = ys(d, 1) - ys(d, -1)
            c = [cut(C[n, k]) for n in range(8)]
            t = (c[0] * cut(xp) + c[1] * cut(xm)) + (c[2] * cut(yp) + c[3] * cut(ym))
            t = t + (c[4] * cut(VV[i, k + 1]) + c[5] * cut(VV[i, k - 1]))
            t = t - c[6] * cut(p) + c[7] * cut(dxy)
            if t.shape == (8, 128):
                T[k, 8:16, 0:128] = t
            else:
                T[k] = t
            return carry

        lax.fori_loop(1, nz + 1, flat, 0)

        pairs = [(j, i + 1) for j in range(i + 2)]

        def deep(k, acc, i=i, cut=cut, last=last, pairs=pairs):
            v = cut(T[k]) + cut(C[8, k]) * (cut(D[k + 1]) - cut(D[k - 1]))
            v = v + cut(C[9, k]) * (cut(E[k + 1]) - cut(E[k - 1]))
            if not last:
                VV[i + 1, k] = v
                v = own(v)
            vs = [own(VV[j, k]) for j in range(i + 1)] + [v]
            return tuple(s + vs[j] * v for s, (j, _) in zip(acc, pairs))

        acc = lax.fori_loop(1, nz + 1, deep, (jnp.zeros((8, 128), F32),) * len(pairs))
        for s, key in zip(acc, pairs):
            sums[key] = s
    line = lanes((1, 128))
    out = jnp.zeros((1, 128), F32)
    for n, key in enumerate(KEYS):
        s = jnp.sum(jnp.sum(sums[key], axis=0, keepdims=True), axis=1, keepdims=True)
        out = jnp.where(line == n, s, out)
    gram[...] = jnp.broadcast_to(out, gram.shape)


KEYS = ((0, 1), (1, 1), (0, 2), (1, 2), (2, 2), (0, 3), (1, 3), (2, 3), (3, 3))


def weights(gram):
    def inner(a, b):
        total = 0.0
        for i in range(4):
            for j in range(4):
                if a[i] is not None and b[j] is not None:
                    total = total + a[i] * b[j] * gram[(min(i, j), max(i, j))]
        return total

    def less(a, s, b):
        out = []
        for one, two in zip(a, b):
            if two is None:
                out.append(one)
            else:
                out.append(-(s * two) if one is None else one - s * two)
        return out

    one = jnp.ones((1, 1), F32)
    r = [one, None, None, None]
    sol = [None] * 4
    dirs, images, norms = [r], [[None, one, None, None]], []
    for n in range(ITERS):
        norms.append(inner(images[n], images[n]))
        beta = inner(r, images[n]) / norms[n]
        sol = less(sol, -beta, dirs[n])
        r = less(r, beta, images[n])
        if n + 1 < ITERS:
            z = [None] + r[:3]
            new_dir, new_img = r, z
            for l in range(n + 1):
                alpha = inner(z, images[l]) / norms[l]
                new_dir = less(new_dir, alpha, dirs[l])
                new_img = less(new_img, alpha, images[l])
            dirs.append(new_dir)
            images.append(new_img)
    return sol[:3]


def last_kernel(partial, moved, basis, dxs, dys, momenta_out, pressure):
    nz = moved.shape[1]
    total = jnp.sum(partial[...], axis=0, keepdims=True)
    line = lanes(total.shape)
    gram = {
        key: jnp.sum(jnp.where(line == n, total, 0.0), axis=1, keepdims=True)
        for n, key in enumerate(KEYS)
    }
    c = [jnp.broadcast_to(s, (8, 128)) for s in weights(gram)]
    p = [(c[0] * basis[0, k] + c[1] * basis[1, k]) + c[2] * basis[2, k] for k in range(nz)]
    h = [0.5 * s for s in c]
    zero = jnp.zeros((8, 128), F32)
    for k in range(nz):
        pressure[k] = p[k]
        dx = (h[0] * dxs[0, k] + h[1] * dxs[1, k]) + h[2] * dxs[2, k]
        dy = (h[0] * dys[0, k] + h[1] * dys[1, k]) + h[2] * dys[2, k]
        above = p[k + 1] if k + 1 < nz else zero
        below = p[k - 1] if k > 0 else zero
        momenta_out[0, k] = moved[0, k] - dx
        momenta_out[1, k] = moved[1, k] - dy
        momenta_out[2, k] = moved[2, k] - 0.5 * (above - below)


def shift_to(a, axis, step):
    n = lax.axis_size(axis)
    return lax.ppermute(a, axis, [(i, (i + step) % n) for i in range(n)])


def local(momenta, theta, courant, density, metric_diag, metric_cross):
    nz = density.shape[0]
    vm = pl.BlockSpec(memory_space=pltpu.VMEM)
    args = (momenta, theta, courant, density, metric_diag, metric_cross)
    sds = jax.ShapeDtypeStruct
    nc = len(COMBOS)
    to_left, to_right, to_up, to_down = pl.pallas_call(
        pack_kernel,
        out_shape=(sds((NF, 8, 128), F32),) * 2 + (sds((nc, nz, 8, 128), F32),) * 2,
        in_specs=[vm] * 6,
        out_specs=[vm] * 4,
        compiler_params=pltpu.CompilerParams(vmem_limit_bytes=16 << 20),
        name="pack",
    )(*args)
    from_left = shift_to(to_right, "gx", 1)
    from_right = shift_to(to_left, "gx", -1)
    below = shift_to(to_up, "gy", 1)
    above = shift_to(to_down, "gy", -1)
    sides = jnp.concatenate((from_left, from_right), axis=0)
    cbelow = shift_to(sides, "gy", 1)
    cabove = shift_to(sides, "gy", -1)

    block = (nz, 8, 128)
    big = (nz + 2, 24, 256)
    nx, ny = lax.axis_size("gx"), lax.axis_size("gy")
    moved, theta_out, basis, dxs, dys, gram = pl.pallas_call(
        main_kernel,
        out_shape=(
            sds((3,) + block, F32),
            sds(block, F32),
            sds((3,) + block, F32),
            sds((3,) + block, F32),
            sds((3,) + block, F32),
            sds((nx, 128), F32),
        ),
        in_specs=[vm] * 12,
        out_specs=[vm] * 6,
        scratch_shapes=[
            pltpu.VMEM((NF,) + big, F32),
            pltpu.VMEM((4,) + big, F32),
            pltpu.VMEM((3,) + big, F32),
            pltpu.VMEM(big, F32),
            pltpu.VMEM((10,) + big, F32),
            pltpu.VMEM((3,) + big, F32),
            pltpu.VMEM(big, F32),
            pltpu.VMEM(big, F32),
            pltpu.VMEM(big, F32),
        ],
        compiler_params=pltpu.CompilerParams(vmem_limit_bytes=40 << 20),
        name="advance",
    )(*args, from_left, from_right, below, above, cbelow, cabove)

    part = lax.all_to_all(gram, "gx", 0, 0, tiled=True)
    part = jnp.broadcast_to(jnp.sum(part, axis=0, keepdims=True), (ny, 128))
    part = lax.all_to_all(part, "gy", 0, 0, tiled=True)

    momenta_out, pressure = pl.pallas_call(
        last_kernel,
        out_shape=(sds((3,) + block, F32), sds(block, F32)),
        in_specs=[vm] * 5,
        out_specs=[vm] * 2,
        compiler_params=pltpu.CompilerParams(vmem_limit_bytes=16 << 20),
        name="combine",
    )(part, moved, basis, dxs, dys)
    return (momenta_out, theta_out, pressure)


def solution(mesh):
    placed = (
        P(None, None, "gy", "gx"),
        P(None, "gy", "gx"),
        P(None, None, "gy", "gx"),
        P(None, "gy", "gx"),
        P(None, None, "gy", "gx"),
        P(None, None, "gy", "gx"),
    )
    return jax.shard_map(
        local,
        mesh=mesh,
        in_specs=placed,
        out_specs=(P(None, None, "gy", "gx"), P(None, "gy", "gx"), P(None, "gy", "gx")),
        check_vma=False,
    )
```

```python
import jax
import jax.numpy as jnp
from jax import lax
from jax.experimental import pallas as pl
from jax.experimental.pallas import tpu as pltpu
from jax.sharding import PartitionSpec as P

helm = 0.02
ITERS = 3
NF = 14
U, V, W, TH, G, CX, CY, CZ, A11, A22, A33, A12, A13, A23 = range(NF)
COMBOS = (
    (V, 6, TH, 2),
    (CY, 6, A12, 2),
    (U, 5, A22, 3),
    (W, 5, A11, 2),
    (G, 5, A33, 2),
    (CX, 5, A13, 2),
    (CZ, 5, A23, 2),
)
F32 = jnp.float32


def lanes(shape):
    return lax.broadcasted_iota(jnp.int32, shape, len(shape) - 1)


def rows(shape):
    return lax.broadcasted_iota(jnp.int32, shape, len(shape) - 2)


def roll(a, shift, axis):
    shift = shift % a.shape[axis]
    if shift == 0:
        return a
    return pltpu.roll(a, shift, axis)


def xs(a, d):
    return roll(a, -d, 1)


def ys(a, d):
    return roll(a, -d, 0)


def field_of(refs, f):
    mom, th, cou, den, dia, cro = refs
    if f < 3:
        return mom.at[f]
    if f == TH:
        return th
    if f == G:
        return den
    if f < 8:
        return cou.at[f - 5]
    if f < 11:
        return dia.at[f - 8]
    return cro.at[f - 11]


def pack_kernel(*refs):
    sources, (to_left, to_right, to_up, to_down) = refs[:6], refs[6:10]
    refs, sem = refs[10:16], refs[16]
    copies = [pltpu.make_async_copy(a, b, sem.at[i]) for i, (a, b) in enumerate(zip(sources, refs))]
    for copy in copies:
        copy.start()
    for copy in copies:
        copy.wait()
    nz = refs[1].shape[0]
    lane = lanes((8, 128)) // 8
    row = rows((8, 128))
    for f in range(NF):
        ref = field_of(refs, f)
        left = jnp.zeros((8, 128), F32)
        right = jnp.zeros((8, 128), F32)
        for k in range(nz):
            moved = roll(ref[k], 8 * k, 1)
            left = jnp.where(lane == k, moved, left)
            right = jnp.where(lane == (k - 1) % nz, moved, right)
        to_left[f] = left
        to_right[f] = right
    for c, (first, n, second, m) in enumerate(COMBOS):
        one, two = field_of(refs, first), field_of(refs, second)
        for k in range(nz):
            a, b = one[k], two[k]
            to_down[c, k] = jnp.where(row < n, a, roll(b, n, 0))
            to_up[c, k] = jnp.where(row >= 8 - n, a, roll(b, -n, 0))


def main_kernel(
    mom, th, cou, den, dia, cro, from_left, from_right, below, above, cbelow, cabove,
    moved, theta_out, basis, dxs, dys, gram,
    S, P1, M, IG, C, VV, D, E, T,
):
    refs = (mom, th, cou, den, dia, cro)
    nz = den.shape[0]
    gy = lax.axis_index("gy")
    ny = lax.axis_size("gy")
    has_below = gy > 0
    has_above = gy < ny - 1
    shape = (24, 256)
    lane128 = lanes((8, 128))
    row24 = rows(shape)
    inside = ((row24 >= 8) | has_below) & ((row24 < 16) | has_above)
    edge_row = ((row24 == 8) & ~has_below) | ((row24 == 16) & ~has_above)

    for c, (first, n, second, m) in enumerate(COMBOS):
        for f, shift in ((first, 0), (second, n)):
            ref = field_of(refs, f)
            outside = 1.0 if f == G else 0.0

            def rows_in(k, carry, f=f, shift=shift, c=c, ref=ref, outside=outside):
                low = roll(below[c, k], shift, 0)
                high = roll(above[c, k], -shift, 0)
                S[f, k + 1, 0:8, 0:128] = jnp.where(has_below, low, outside)
                S[f, k + 1, 8:16, 0:128] = ref[k]
                S[f, k + 1, 16:24, 0:128] = jnp.where(has_above, high, outside)
                return carry

            lax.fori_loop(0, nz, rows_in, 0, unroll=True)
    for f in range(NF):
        outside = 1.0 if f == G else 0.0
        for g, (left, right) in enumerate(
            (
                (cbelow[f], cbelow[NF + f]),
                (from_left[f], from_right[f]),
                (cabove[f], cabove[NF + f]),
            )
        ):
            if g == 0:
                left, right = (jnp.where(has_below, a, outside) for a in (left, right))
            if g == 2:
                left, right = (jnp.where(has_above, a, outside) for a in (left, right))
            for k in range(nz):
                S[f, k + 1, 8 * g : 8 * g + 8, 128:256] = jnp.where(
                    lane128 < 64, roll(right, -8 * k, 1), roll(left, -8 * k, 1)
                )
        pad = jnp.full(shape, outside, F32)
        S[f, 0] = pad
        S[f, nz + 1] = pad
    zero = jnp.zeros(shape, F32)
    S[CZ, 1] = zero

    def upwind(k, fz):
        cx, cy, cz = S[CX, k], S[CY, k], S[CZ, k + 1]
        cy = jnp.where(edge_row, 0.0, cy)
        S[CY, k] = cy
        ig = 1.0 / S[G, k]
        IG[k] = ig
        xp, xm = jnp.maximum(cx, 0.0), jnp.minimum(cx, 0.0)
        yp, ym = jnp.maximum(cy, 0.0), jnp.minimum(cy, 0.0)
        zp, zm = jnp.maximum(cz, 0.0), jnp.minimum(cz, 0.0)
        out = []
        for f in range(4):
            psi = S[f, k]
            fx = xp * xs(psi, -1) + xm * psi
            fy = yp * ys(psi, -1) + ym * psi
            up = zp * psi + zm * S[f, k + 1]
            P1[f, k] = psi - (xs(fx, 1) - fx + ys(fy, 1) - fy + up - fz[f]) * ig
            out.append(up)
        return tuple(out)

    lax.fori_loop(1, nz + 1, upwind, (zero,) * 4, unroll=4)
    for f in range(4):
        P1[f, 0] = zero
        P1[f, nz + 1] = zero

    def face(c, one, two):
        return 0.5 * (jnp.abs(c) - c * c / (0.5 * (one + two)))

    def anti(k, az):
        dens = S[G, k]
        kx = face(S[CX, k], xs(dens, -1), dens)
        ky = face(S[CY, k], ys(dens, -1), dens)
        kz = face(S[CZ, k + 1], dens, S[G, k + 1])
        ig = IG[k]
        out = []
        for f in range(4):
            psi = P1[f, k]
            ax = kx * (psi - xs(psi, -1))
            ay = ky * (psi - ys(psi, -1))
            up = kz * (P1[f, k + 1] - psi)
            res = psi - (xs(ax, 1) - ax + ys(ay, 1) - ay + up - az[f]) * ig
            if f < 3:
                M[f, k] = res
                moved[f, k - 1] = res[8:16, 0:128]
            else:
                theta_out[k - 1] = res[8:16, 0:128]
            out.append(up)
        return tuple(out)

    lax.fori_loop(1, nz + 1, anti, (zero,) * 4, unroll=4)
    M[2, 0] = zero
    M[2, nz + 1] = zero

    def first(k, carry):
        u, v = M[0, k], M[1, k]
        rhs = 0.5 * (
            (xs(u, 1) - xs(u, -1)) + (ys(v, 1) - ys(v, -1)) + (M[2, k + 1] - M[2, k - 1])
        )
        VV[0, k] = jnp.where(inside, rhs, 0.0)
        a11, a22, a33 = S[A11, k], S[A22, k], S[A33, k]
        wxl = 0.5 * (xs(a11, -1) + a11)
        wyl = jnp.where(edge_row, 0.0, 0.5 * (ys(a22, -1) + a22))
        wzl = jnp.where(k > 1, 0.5 * (S[A33, k - 1] + a33), 0.0)
        wz = jnp.where(k < nz, 0.5 * (S[A33, k + 1] + a33), 0.0)
        wx, wy = xs(wxl, 1), ys(wyl, 1)
        C[0, k] = wx
        C[1, k] = wxl
        C[2, k] = wy
        C[3, k] = wyl
        C[4, k] = wz
        C[5, k] = wzl
        C[6, k] = ((wx + wxl) + (wy + wyl)) + ((wz + wzl) + helm)
        C[7, k] = 0.25 * S[A12, k]
        C[8, k] = 0.25 * S[A13, k]
        C[9, k] = 0.25 * S[A23, k]
        return carry

    lax.fori_loop(1, nz + 1, first, 0, unroll=4)
    for i in range(3):
        VV[i, 0] = zero
        VV[i, nz + 1] = zero
    for a in (D, E):
        a[0] = zero
        a[nz + 1] = zero

    own = lambda a: a[8:16, 0:128]
    sums = {}
    for i in range(3):
        last = i == 2
        cut = own if last else (lambda a: a)

        def flat(k, carry, i=i, cut=cut):
            p = VV[i, k]
            xp, xm, yp, ym = xs(p, 1), xs(p, -1), ys(p, 1), ys(p, -1)
            d, e = xp - xm, yp - ym
            D[k] = d
            E[k] = e
            dxs[i, k - 1] = own(d)
            dys[i, k - 1] = own(e)
            basis[i, k - 1] = own(p)
            dxy = ys(d, 1) - ys(d, -1)
            c = [cut(C[n, k]) for n in range(8)]
            t = (c[0] * cut(xp) + c[1] * cut(xm)) + (c[2] * cut(yp) + c[3] * cut(ym))
            t = t + (c[4] * cut(VV[i, k + 1]) + c[5] * cut(VV[i, k - 1]))
            t = t - c[6] * cut(p) + c[7] * cut(dxy)
            if t.shape == (8, 128):
                T[k, 8:16, 0:128] = t
            else:
                T[k] = t
            return carry

        lax.fori_loop(1, nz + 1, flat, 0, unroll=4)

        pairs = [(j, i + 1) for j in range(i + 2)]

        def deep(k, acc, i=i, cut=cut, last=last, pairs=pairs):
            v = cut(T[k]) + cut(C[8, k]) * (cut(D[k + 1]) - cut(D[k - 1]))
            v = v + cut(C[9, k]) * (cut(E[k + 1]) - cut(E[k - 1]))
            if not last:
                VV[i + 1, k] = v
                v = own(v)
            vs = [own(VV[j, k]) for j in range(i + 1)] + [v]
            return tuple(s + vs[j] * v for s, (j, _) in zip(acc, pairs))

        start = (jnp.zeros((8, 128), F32),) * len(pairs)
        acc = lax.fori_loop(1, nz + 1, deep, start, unroll=4)
        for s, key in zip(acc, pairs):
            sums[key] = s
    line = lanes((1, 128))
    out = jnp.zeros((1, 128), F32)
    for n, key in enumerate(KEYS):
        s = jnp.sum(jnp.sum(sums[key], axis=0, keepdims=True), axis=1, keepdims=True)
        out = jnp.where(line == n, s, out)
    gram[...] = jnp.broadcast_to(out, gram.shape)


KEYS = ((0, 1), (1, 1), (0, 2), (1, 2), (2, 2), (0, 3), (1, 3), (2, 3), (3, 3))


def weights(gram):
    def inner(a, b):
        total = 0.0
        for i in range(4):
            for j in range(4):
                if a[i] is not None and b[j] is not None:
                    total = total + a[i] * b[j] * gram[(min(i, j), max(i, j))]
        return total

    def less(a, s, b):
        out = []
        for one, two in zip(a, b):
            if two is None:
                out.append(one)
            else:
                out.append(-(s * two) if one is None else one - s * two)
        return out

    one = jnp.ones((1, 1), F32)
    r = [one, None, None, None]
    sol = [None] * 4
    dirs, images, norms = [r], [[None, one, None, None]], []
    for n in range(ITERS):
        norms.append(inner(images[n], images[n]))
        beta = inner(r, images[n]) / norms[n]
        sol = less(sol, -beta, dirs[n])
        r = less(r, beta, images[n])
        if n + 1 < ITERS:
            z = [None] + r[:3]
            new_dir, new_img = r, z
            for l in range(n + 1):
                alpha = inner(z, images[l]) / norms[l]
                new_dir = less(new_dir, alpha, dirs[l])
                new_img = less(new_img, alpha, images[l])
            dirs.append(new_dir)
            images.append(new_img)
    return sol[:3]


def last_kernel(partial, moved, basis, dxs, dys, momenta_out, pressure):
    nz = moved.shape[1]
    total = jnp.sum(partial[...], axis=0, keepdims=True)
    line = lanes(total.shape)
    gram = {
        key: jnp.sum(jnp.where(line == n, total, 0.0), axis=1, keepdims=True)
        for n, key in enumerate(KEYS)
    }
    c = [jnp.broadcast_to(s, (8, 128)) for s in weights(gram)]
    p = [(c[0] * basis[0, k] + c[1] * basis[1, k]) + c[2] * basis[2, k] for k in range(nz)]
    h = [0.5 * s for s in c]
    zero = jnp.zeros((8, 128), F32)
    for k in range(nz):
        pressure[k] = p[k]
        dx = (h[0] * dxs[0, k] + h[1] * dxs[1, k]) + h[2] * dxs[2, k]
        dy = (h[0] * dys[0, k] + h[1] * dys[1, k]) + h[2] * dys[2, k]
        above = p[k + 1] if k + 1 < nz else zero
        below = p[k - 1] if k > 0 else zero
        momenta_out[0, k] = moved[0, k] - dx
        momenta_out[1, k] = moved[1, k] - dy
        momenta_out[2, k] = moved[2, k] - 0.5 * (above - below)


def shift_to(a, axis, step):
    n = lax.axis_size(axis)
    return lax.ppermute(a, axis, [(i, (i + step) % n) for i in range(n)])


def local(momenta, theta, courant, density, metric_diag, metric_cross):
    nz = density.shape[0]
    vm = pl.BlockSpec(memory_space=pltpu.VMEM)
    args = (momenta, theta, courant, density, metric_diag, metric_cross)
    sds = jax.ShapeDtypeStruct
    nc = len(COMBOS)
    to_left, to_right, to_up, to_down = pl.pallas_call(
        pack_kernel,
        out_shape=(sds((NF, 8, 128), F32),) * 2 + (sds((nc, nz, 8, 128), F32),) * 2,
        in_specs=[pl.BlockSpec(memory_space=pltpu.HBM)] * 6,
        out_specs=[vm] * 4,
        scratch_shapes=[pltpu.VMEM(a.shape, F32) for a in args] + [pltpu.SemaphoreType.DMA((6,))],
        compiler_params=pltpu.CompilerParams(vmem_limit_bytes=16 << 20),
        name="pack",
    )(*(pltpu.with_memory_space_constraint(a, pltpu.HBM) for a in args))
    from_left = shift_to(to_right, "gx", 1)
    from_right = shift_to(to_left, "gx", -1)
    below = shift_to(to_up, "gy", 1)
    above = shift_to(to_down, "gy", -1)
    sides = jnp.concatenate((from_left, from_right), axis=0)
    cbelow = shift_to(sides, "gy", 1)
    cabove = shift_to(sides, "gy", -1)

    block = (nz, 8, 128)
    big = (nz + 2, 24, 256)
    nx, ny = lax.axis_size("gx"), lax.axis_size("gy")
    moved, theta_out, basis, dxs, dys, gram = pl.pallas_call(
        main_kernel,
        out_shape=(
            sds((3,) + block, F32),
            sds(block, F32),
            sds((3,) + block, F32),
            sds((3,) + block, F32),
            sds((3,) + block, F32),
            sds((nx, 128), F32),
        ),
        in_specs=[vm] * 12,
        out_specs=[vm] * 6,
        scratch_shapes=[
            pltpu.VMEM((NF,) + big, F32),
            pltpu.VMEM((4,) + big, F32),
            pltpu.VMEM((3,) + big, F32),
            pltpu.VMEM(big, F32),
            pltpu.VMEM((10,) + big, F32),
            pltpu.VMEM((3,) + big, F32),
            pltpu.VMEM(big, F32),
            pltpu.VMEM(big, F32),
            pltpu.VMEM(big, F32),
        ],
        compiler_params=pltpu.CompilerParams(vmem_limit_bytes=40 << 20),
        name="advance",
    )(*args, from_left, from_right, below, above, cbelow, cabove)

    part = lax.all_to_all(gram, "gx", 0, 0, tiled=True)
    part = jnp.broadcast_to(jnp.sum(part, axis=0, keepdims=True), (ny, 128))
    part = lax.all_to_all(part, "gy", 0, 0, tiled=True)

    momenta_out, pressure = pl.pallas_call(
        last_kernel,
        out_shape=(sds((3,) + block, F32), sds(block, F32)),
        in_specs=[vm] * 5,
        out_specs=[vm] * 2,
        compiler_params=pltpu.CompilerParams(vmem_limit_bytes=16 << 20),
        name="combine",
    )(part, moved, basis, dxs, dys)
    return (momenta_out, theta_out, pressure)


def solution(mesh):
    placed = (
        P(None, None, "gy", "gx"),
        P(None, "gy", "gx"),
        P(None, None, "gy", "gx"),
        P(None, "gy", "gx"),
        P(None, None, "gy", "gx"),
        P(None, None, "gy", "gx"),
    )
    return jax.shard_map(
        local,
        mesh=mesh,
        in_specs=placed,
        out_specs=(P(None, None, "gy", "gx"), P(None, "gy", "gx"), P(None, "gy", "gx")),
        check_vma=False,
    )
```

```python
import jax
import jax.numpy as jnp
from jax import lax
from jax.experimental import pallas as pl
from jax.experimental.pallas import tpu as pltpu
from jax.sharding import PartitionSpec as P

helm = 0.02
ITERS = 3
NF = 14
U, V, W, TH, G, CX, CY, CZ, A11, A22, A33, A12, A13, A23 = range(NF)
COMBOS = (
    (V, 6, TH, 2),
    (CY, 6, A12, 2),
    (U, 5, A22, 3),
    (W, 5, A11, 2),
    (G, 5, A33, 2),
    (CX, 5, A13, 2),
    (CZ, 5, A23, 2),
)
F32 = jnp.float32


def lanes(shape):
    return lax.broadcasted_iota(jnp.int32, shape, len(shape) - 1)


def rows(shape):
    return lax.broadcasted_iota(jnp.int32, shape, len(shape) - 2)


def roll(a, shift, axis):
    shift = shift % a.shape[axis]
    if shift == 0:
        return a
    return pltpu.roll(a, shift, axis)


def xs(a, d):
    return roll(a, -d, 1)


def ys(a, d):
    return roll(a, -d, 0)


def rim_x(q, d):
    c = lanes((48, 128)) % 8
    moved = roll(q, -d, 1)
    if d > 0:
        first = jnp.where(c == 7, roll(q[48:], 7, 1), moved[:48])
        return jnp.concatenate((first, moved[48:]), axis=0)
    last = jnp.where(c == 0, roll(q[:48], -7, 1), moved[48:])
    return jnp.concatenate((moved[:48], last), axis=0)


def rim_z(q, d):
    lane = lanes(q.shape)
    end = lane >= 120 if d > 0 else lane < 8
    return jnp.where(end, 0.0, roll(q, -8 * d, 1))


def rim_own(q):
    return jnp.where(lanes((8, 128)) % 8 < 4, q[56:64], q[32:40])


def upwind_weights(cx, cr, cy, cd, cz, cu, dens):
    ig = 1.0 / dens
    pos, neg = (lambda a: jnp.maximum(a, 0.0)), (lambda a: jnp.minimum(a, 0.0))
    rp, rn, lp, ln = pos(cr), neg(cr), pos(cx), neg(cx)
    dp, dn, up, un = pos(cd), neg(cd), pos(cy), neg(cy)
    ap, an, bp, bn = pos(cu), neg(cu), pos(cz), neg(cz)
    mid = 1.0 - ig * (((rp - ln) + (dp - un)) + (ap - bn))
    return mid, tuple(ig * a for a in (lp, -rn, up, -dn, bp, -an)), ig


def face(c, one, two):
    return 0.5 * (jnp.abs(c) - c * c / (0.5 * (one + two)))


def anti_weights(faces, ig):
    kl, kr, ku, kd, kb, ka = faces
    mid = 1.0 + ig * (((kl + kr) + (ku + kd)) + (ka + kb))
    return mid, tuple(-ig * a for a in faces)


def seven(mid, w, p, around):
    x = w[0] * around[0] + w[1] * around[1]
    y = w[2] * around[2] + w[3] * around[3]
    z = w[4] * around[4] + w[5] * around[5]
    return (mid * p + x) + (y + z)


def field_of(refs, f):
    mom, th, cou, den, dia, cro = refs
    if f < 3:
        return mom.at[f]
    if f == TH:
        return th
    if f == G:
        return den
    if f < 8:
        return cou.at[f - 5]
    if f < 11:
        return dia.at[f - 8]
    return cro.at[f - 11]


def fetch_kernel(*refs):
    sources, refs, (to_up, to_down, sem) = refs[:6], refs[6:12], refs[12:]
    copies = [pltpu.make_async_copy(a, b, sem.at[i]) for i, (a, b) in enumerate(zip(sources, refs))]
    for copy in copies:
        copy.start()
    for copy in copies:
        copy.wait()
    cou = refs[2]
    nz = refs[1].shape[0]
    row = rows((8, 128))
    first_row = (row == 0) & (lax.axis_index("gy") == 0)
    for k in range(nz):
        cou[1, k] = jnp.where(first_row, 0.0, cou[1, k])
    cou[2, 0] = jnp.zeros((8, 128), F32)
    for c, (first, n, second, m) in enumerate(COMBOS):
        one, two = field_of(refs, first), field_of(refs, second)
        for k in range(nz):
            a, b = one[k], two[k]
            to_down[c, k] = jnp.where(row < n, a, roll(b, n, 0))
            to_up[c, k] = jnp.where(row >= 8 - n, a, roll(b, -n, 0))


def strips_kernel(mom, th, cou, den, dia, cro, below, above, S, to_left, to_right):
    refs = (mom, th, cou, den, dia, cro)
    nz = den.shape[0]
    gy = lax.axis_index("gy")
    has_below = gy > 0
    has_above = gy < lax.axis_size("gy") - 1
    slot = lanes((24, 128)) // 8
    for c, (first, n, second, m) in enumerate(COMBOS):
        for f, shift in ((first, 0), (second, n)):
            ref = field_of(refs, f)
            outside = 1.0 if f == G else 0.0
            left = jnp.zeros((24, 128), F32)
            right = jnp.zeros((24, 128), F32)
            for k in range(nz):
                low = jnp.where(has_below, roll(below[c, k], shift, 0), outside)
                high = jnp.where(has_above, roll(above[c, k], -shift, 0), outside)
                whole = jnp.concatenate((low, ref[k], high), axis=0)
                S[f, k + 1] = whole
                moved = roll(whole, 8 * k, 1)
                left = jnp.where(slot == k, moved, left)
                right = jnp.where(slot == (k - 1) % nz, moved, right)
            to_left[f] = left
            to_right[f] = roll(right, 8, 1)
            pad = jnp.full((24, 128), outside, F32)
            S[f, 0] = pad
            S[f, nz + 1] = pad


def masks(shape):
    gy = lax.axis_index("gy")
    has_below = gy > 0
    has_above = gy < lax.axis_size("gy") - 1
    row = rows(shape) % 24
    inside = ((row >= 8) | has_below) & ((row < 16) | has_above)
    edge = ((row == 8) & ~has_below) | ((row == 16) & ~has_above)
    return inside, edge


def core_kernel(S, moved, right_side, C, P1, M):
    nz = moved.shape[1]
    shape = (24, 128)
    inside, edge = masks(shape)
    zero = jnp.zeros(shape, F32)

    def upwind(k, carry):
        cx, cy, cz, cu = S[CX, k], S[CY, k], S[CZ, k], S[CZ, k + 1]
        mid, w, ig = upwind_weights(cx, xs(cx, 1), cy, ys(cy, 1), cz, cu, S[G, k])
        for f in range(4):
            psi = S[f, k]
            around = (xs(psi, -1), xs(psi, 1), ys(psi, -1), ys(psi, 1), S[f, k - 1], S[f, k + 1])
            P1[f, k] = seven(mid, w, psi, around)
        return carry

    lax.fori_loop(1, nz + 1, upwind, 0, unroll=4)
    for f in range(4):
        P1[f, 0] = zero
        P1[f, nz + 1] = zero

    def anti(k, kb):
        dens = S[G, k]
        kl = face(S[CX, k], xs(dens, -1), dens)
        ku = face(S[CY, k], ys(dens, -1), dens)
        ka = face(S[CZ, k + 1], dens, S[G, k + 1])
        mid, w = anti_weights((kl, xs(kl, 1), ku, ys(ku, 1), kb, ka), 1.0 / dens)
        for f in range(4):
            psi = P1[f, k]
            around = (xs(psi, -1), xs(psi, 1), ys(psi, -1), ys(psi, 1), P1[f, k - 1], P1[f, k + 1])
            res = seven(mid, w, psi, around)
            if f < 3:
                M[f, k] = res
            moved[f, k - 1] = res[8:16]
        return ka

    lax.fori_loop(1, nz + 1, anti, zero, unroll=4)
    M[2, 0] = zero
    M[2, nz + 1] = zero

    def first(k, carry):
        u, v = M[0, k], M[1, k]
        rhs = 0.5 * (
            (xs(u, 1) - xs(u, -1)) + (ys(v, 1) - ys(v, -1)) + (M[2, k + 1] - M[2, k - 1])
        )
        right_side[k - 1] = jnp.where(inside, rhs, 0.0)
        a11, a22, a33 = S[A11, k], S[A22, k], S[A33, k]
        wxl = 0.5 * (xs(a11, -1) + a11)
        wyl = jnp.where(edge, 0.0, 0.5 * (ys(a22, -1) + a22))
        wzl = jnp.where(k > 1, 0.5 * (S[A33, k - 1] + a33), 0.0)
        wz = jnp.where(k < nz, 0.5 * (S[A33, k + 1] + a33), 0.0)
        wx, wy = xs(wxl, 1), ys(wyl, 1)
        for n, w in enumerate((wx, wxl, wy, wyl, wz, wzl)):
            C[n, k - 1] = w
        C[6, k - 1] = ((wx + wxl) + (wy + wyl)) + ((wz + wzl) + helm)
        C[7, k - 1] = 0.25 * S[A12, k]
        C[8, k - 1] = 0.25 * S[A13, k]
        C[9, k - 1] = 0.25 * S[A23, k]
        return carry

    lax.fori_loop(1, nz + 1, first, 0, unroll=4)


def solve_kernel(
    right_side, C, to_left, to_right, from_left, from_right,
    basis, dxs, dys, rim_moved, rim_basis, rim_dxs, rim_dys, gram,
    VV, D, E, T,
):
    nz = right_side.shape[0]
    shape = (24, 128)
    zero = jnp.zeros(shape, F32)
    inside, edge = masks((96, 128))
    lane96 = lanes((96, 128))

    def rim_field(f):
        return jnp.concatenate((from_left[f], to_right[f], to_left[f], from_right[f]), axis=0)

    def around(q):
        return (
            rim_x(q, -1), rim_x(q, 1), ys(q, -1), ys(q, 1), rim_z(q, -1), rim_z(q, 1)
        )

    cx, cy, cz, dens = rim_field(CX), rim_field(CY), rim_field(CZ), rim_field(G)
    cu = rim_z(cz, 1)
    mid, w, ig = upwind_weights(cx, rim_x(cx, 1), cy, ys(cy, 1), cz, cu, dens)
    kl = face(cx, rim_x(dens, -1), dens)
    ku = face(cy, ys(dens, -1), dens)
    kb = face(cz, roll(dens, 8, 1), dens)
    mid2, w2 = anti_weights((kl, rim_x(kl, 1), ku, ys(ku, 1), kb, rim_z(kb, 1)), ig)
    done = []
    for f in range(4):
        psi = rim_field(f)
        psi = seven(mid, w, psi, around(psi))
        psi = seven(mid2, w2, psi, around(psi))
        rim_moved[f] = rim_own(psi)
        done.append(psi)
    u, v, t = done[:3]
    v0 = 0.5 * (
        (rim_x(u, 1) - rim_x(u, -1)) + (ys(v, 1) - ys(v, -1)) + (rim_z(t, 1) - rim_z(t, -1))
    )
    v0 = jnp.where(inside, v0, 0.0)

    lane = lanes(shape)
    c24 = lane % 8
    slot = lane // 8
    edges = jnp.where(c24 < 4, v0[48:72], v0[24:48])
    turned = [roll(edges, -8 * k, 1) for k in range(nz)]
    inner = zero
    for k in range(nz):
        core = right_side[k]
        VV[0, k + 1] = jnp.where(
            lane < 4, turned[k], jnp.where(lane >= 124, turned[(k + 1) % nz], core)
        )
        take = ((slot == k) & (c24 >= 4)) | ((slot == (k - 1) % nz) & (c24 < 4))
        inner = jnp.where(take, roll(core, 8 * k, 1), inner)
    q = jnp.concatenate(
        (
            v0[0:24],
            jnp.where(c24 < 4, roll(inner, 8, 1), v0[24:48]),
            jnp.where(c24 >= 4, inner, v0[48:72]),
            v0[72:96],
        ),
        axis=0,
    )

    a11, a22, a33 = rim_field(A11), rim_field(A22), rim_field(A33)
    wxl = 0.5 * (rim_x(a11, -1) + a11)
    wyl = jnp.where(edge, 0.0, 0.5 * (ys(a22, -1) + a22))
    wzl = jnp.where(lane96 < 8, 0.0, 0.5 * (roll(a33, 8, 1) + a33))
    wx, wy, wz = rim_x(wxl, 1), ys(wyl, 1), rim_z(wzl, 1)
    wc = ((wx + wxl) + (wy + wyl)) + ((wz + wzl) + helm)
    q12, q13, q23 = (0.25 * rim_field(f) for f in (A12, A13, A23))
    rims = [rim_own(q)]
    rim_basis[0] = rims[0]
    for i in range(3):
        xm, xp, ym, yp, zm, zp = around(q)
        d, e = xp - xm, yp - ym
        rim_dxs[i] = rim_own(d)
        rim_dys[i] = rim_own(e)
        new = seven(-wc, (wxl, wx, wyl, wy, wzl, wz), q, (xm, xp, ym, yp, zm, zp))
        new = new + q12 * (ys(d, 1) - ys(d, -1))
        new = new + q13 * (rim_z(d, 1) - rim_z(d, -1))
        q = new + q23 * (rim_z(e, 1) - rim_z(e, -1))
        rims.append(rim_own(q))
        if i < 2:
            rim_basis[i + 1] = rims[-1]

    for i in range(3):
        VV[i, 0] = zero
        VV[i, nz + 1] = zero
    for a in (D, E):
        a[0] = zero
        a[nz + 1] = zero
    own = lambda a: a[8:16]
    sums = {}
    for i in range(3):
        last = i == 2
        cut = own if last else (lambda a: a)

        def flat(k, carry, i=i, cut=cut, last=last):
            p = VV[i, k]
            xp, xm, yp, ym = xs(p, 1), xs(p, -1), ys(p, 1), ys(p, -1)
            d, e = xp - xm, yp - ym
            D[k] = d
            E[k] = e
            dxs[i, k - 1] = own(d)
            dys[i, k - 1] = own(e)
            basis[i, k - 1] = own(p)
            near = (xp, xm, yp, ym, VV[i, k + 1], VV[i, k - 1])
            t = seven(-cut(C[6, k - 1]), [cut(C[n, k - 1]) for n in range(6)], cut(p), [cut(a) for a in near])
            t = t + cut(C[7, k - 1]) * cut(ys(d, 1) - ys(d, -1))
            if last:
                T[k, 8:16] = t
            else:
                T[k] = t
            return carry

        lax.fori_loop(1, nz + 1, flat, 0, unroll=4)
        pairs = [(j, i + 1) for j in range(i + 2)]

        def deep(k, acc, i=i, cut=cut, last=last, pairs=pairs):
            v = cut(T[k]) + cut(C[8, k - 1]) * (cut(D[k + 1]) - cut(D[k - 1]))
            v = v + cut(C[9, k - 1]) * (cut(E[k + 1]) - cut(E[k - 1]))
            if not last:
                VV[i + 1, k] = v
                v = own(v)
            vs = [own(VV[j, k]) for j in range(i + 1)] + [v]
            return tuple(s + vs[j] * v for s, (j, _) in zip(acc, pairs))

        start = (jnp.zeros((8, 128), F32),) * len(pairs)
        acc = lax.fori_loop(1, nz + 1, deep, start, unroll=4)
        for s, key in zip(acc, pairs):
            sums[key] = s
    lane8 = lanes((8, 128))
    core_part = (lane8 >= 4) & (lane8 < 124)
    line = lanes((1, 128))
    out = jnp.zeros((1, 128), F32)
    for n, (i, j) in enumerate(KEYS):
        s = jnp.where(core_part, sums[(i, j)], 0.0) + rims[i] * rims[j]
        s = jnp.sum(jnp.sum(s, axis=0, keepdims=True), axis=1, keepdims=True)
        out = jnp.where(line == n, s, out)
    gram[...] = jnp.broadcast_to(out, gram.shape)


KEYS = ((0, 1), (1, 1), (0, 2), (1, 2), (2, 2), (0, 3), (1, 3), (2, 3), (3, 3))


def weights(gram):
    def inner(a, b):
        total = 0.0
        for i in range(4):
            for j in range(4):
                if a[i] is not None and b[j] is not None:
                    total = total + a[i] * b[j] * gram[(min(i, j), max(i, j))]
        return total

    def less(a, s, b):
        out = []
        for one, two in zip(a, b):
            if two is None:
                out.append(one)
            else:
                out.append(-(s * two) if one is None else one - s * two)
        return out

    one = jnp.ones((1, 1), F32)
    r = [one, None, None, None]
    sol = [None] * 4
    dirs, images, norms = [r], [[None, one, None, None]], []
    for n in range(ITERS):
        norms.append(inner(images[n], images[n]))
        beta = inner(r, images[n]) / norms[n]
        sol = less(sol, -beta, dirs[n])
        r = less(r, beta, images[n])
        if n + 1 < ITERS:
            z = [None] + r[:3]
            new_dir, new_img = r, z
            for l in range(n + 1):
                alpha = inner(z, images[l]) / norms[l]
                new_dir = less(new_dir, alpha, dirs[l])
                new_img = less(new_img, alpha, images[l])
            dirs.append(new_dir)
            images.append(new_img)
    return sol[:3]


def last_kernel(
    partial, moved, basis, dxs, dys, rim_moved, rim_basis, rim_dxs, rim_dys,
    momenta_out, theta_out, pressure,
):
    nz = moved.shape[1]
    total = jnp.sum(partial[...], axis=0, keepdims=True)
    line = lanes(total.shape)
    gram = {
        key: jnp.sum(jnp.where(line == n, total, 0.0), axis=1, keepdims=True)
        for n, key in enumerate(KEYS)
    }
    c = [jnp.broadcast_to(s, (8, 128)) for s in weights(gram)]
    h = [0.5 * s for s in c]
    lane = lanes((8, 128))

    def mix(s, a):
        return (s[0] * a[0] + s[1] * a[1]) + s[2] * a[2]

    def joined(rim, core):
        turned = [roll(rim, -8 * k, 1) for k in range(nz)]
        return [
            jnp.where(lane < 4, turned[k], jnp.where(lane >= 124, turned[(k + 1) % nz], core[k]))
            for k in range(nz)
        ]

    p_rim = mix(c, rim_basis)
    p = joined(p_rim, [mix(c, [basis[i, k] for i in range(3)]) for k in range(nz)])
    for k in range(nz):
        pressure[k] = p[k]
    zero = jnp.zeros((8, 128), F32)
    for n, (diff, rim_diff) in enumerate(((dxs, rim_dxs), (dys, rim_dys))):
        core = [moved[n, k] - mix(h, [diff[i, k] for i in range(3)]) for k in range(nz)]
        for k, a in enumerate(joined(rim_moved[n] - mix(h, rim_diff), core)):
            momenta_out[n, k] = a
    for k, a in enumerate(joined(rim_moved[2], [moved[2, k] for k in range(nz)])):
        above = p[k + 1] if k + 1 < nz else zero
        below = p[k - 1] if k > 0 else zero
        momenta_out[2, k] = a - 0.5 * (above - below)
    for k, a in enumerate(joined(rim_moved[3], [moved[3, k] for k in range(nz)])):
        theta_out[k] = a


def shift_to(a, axis, step):
    n = lax.axis_size(axis)
    return lax.ppermute(a, axis, [(i, (i + step) % n) for i in range(n)])


def call(kernel, name, out, scratch=(), space=pltpu.VMEM, limit=16):
    def run(*args):
        return pl.pallas_call(
            kernel,
            out_shape=tuple(jax.ShapeDtypeStruct(a, F32) for a in out),
            in_specs=[pl.BlockSpec(memory_space=space)] * len(args),
            out_specs=[pl.BlockSpec(memory_space=pltpu.VMEM)] * len(out),
            scratch_shapes=list(scratch),
            compiler_params=pltpu.CompilerParams(vmem_limit_bytes=limit << 20),
            name=name,
        )(*args)

    return run


def local(momenta, theta, courant, density, metric_diag, metric_cross):
    nz = density.shape[0]
    args = (momenta, theta, courant, density, metric_diag, metric_cross)
    block = (nz, 8, 128)
    core = (nz, 24, 128)
    deep = (nz + 2, 24, 128)
    nx, ny = lax.axis_size("gx"), lax.axis_size("gy")
    rows_out = (len(COMBOS), nz, 8, 128)

    *args, to_up, to_down = call(
        fetch_kernel,
        "fetch",
        [a.shape for a in args] + [rows_out] * 2,
        [pltpu.SemaphoreType.DMA((6,))],
        pltpu.HBM,
    )(*(pltpu.with_memory_space_constraint(a, pltpu.HBM) for a in args))
    below = shift_to(to_up, "gy", 1)
    above = shift_to(to_down, "gy", -1)
    S, to_left, to_right = call(
        strips_kernel, "strips", [(NF,) + deep] + [(NF, 24, 128)] * 2
    )(*args, below, above)
    from_left = shift_to(to_right, "gx", 1)
    from_right = shift_to(to_left, "gx", -1)
    moved, right_side, coef = call(
        core_kernel,
        "core",
        [(4,) + block, core, (10,) + core],
        [pltpu.VMEM((4,) + deep, F32), pltpu.VMEM((3,) + deep, F32)],
    )(S)
    three, rim = (3,) + block, (3, 8, 128)
    *parts, gram = call(
        solve_kernel,
        "solve",
        [three] * 3 + [(4, 8, 128), rim, rim, rim, (nx, 128)],
        [pltpu.VMEM((3,) + deep, F32)] + [pltpu.VMEM(deep, F32)] * 3,
    )(right_side, coef, to_left, to_right, from_left, from_right)

    part = lax.all_to_all(gram, "gx", 0, 0, tiled=True)
    part = jnp.broadcast_to(jnp.sum(part, axis=0, keepdims=True), (ny, 128))
    part = lax.all_to_all(part, "gy", 0, 0, tiled=True)
    momenta_out, theta_out, pressure = call(
        last_kernel, "combine", [three, block, block]
    )(part, moved, *parts)
    return (momenta_out, theta_out, pressure)


def solution(mesh):
    placed = (
        P(None, None, "gy", "gx"),
        P(None, "gy", "gx"),
        P(None, None, "gy", "gx"),
        P(None, "gy", "gx"),
        P(None, None, "gy", "gx"),
        P(None, None, "gy", "gx"),
    )
    return jax.shard_map(
        local,
        mesh=mesh,
        in_specs=placed,
        out_specs=(P(None, None, "gy", "gx"), P(None, "gy", "gx"), P(None, "gy", "gx")),
        check_vma=False,
    )
```

```python
import jax
import jax.numpy as jnp
from jax import lax
from jax.experimental import pallas as pl
from jax.experimental.pallas import tpu as pltpu
from jax.sharding import PartitionSpec as P

helm = 0.02
ITERS = 3
NF = 14
U, V, W, TH, G, CX, CY, CZ, A11, A22, A33, A12, A13, A23 = range(NF)
COMBOS = (
    (V, 6, TH, 2),
    (CY, 6, A12, 2),
    (U, 5, A22, 3),
    (W, 5, A11, 2),
    (G, 5, A33, 2),
    (CX, 5, A13, 2),
    (CZ, 5, A23, 2),
)
F32 = jnp.float32


def lanes(shape):
    return lax.broadcasted_iota(jnp.int32, shape, len(shape) - 1)


def rows(shape):
    return lax.broadcasted_iota(jnp.int32, shape, len(shape) - 2)


def roll(a, shift, axis):
    shift = shift % a.shape[axis]
    if shift == 0:
        return a
    return pltpu.roll(a, shift, axis)


def xs(a, d):
    return roll(a, -d, 1)


def ys(a, d):
    return roll(a, -d, 0)


def rim_x(q, d):
    c = lanes((48, 128)) % 8
    moved = roll(q, -d, 1)
    if d > 0:
        first = jnp.where(c == 7, roll(q[48:], 7, 1), moved[:48])
        return jnp.concatenate((first, moved[48:]), axis=0)
    last = jnp.where(c == 0, roll(q[:48], -7, 1), moved[48:])
    return jnp.concatenate((moved[:48], last), axis=0)


def rim_z(q, d):
    lane = lanes(q.shape)
    end = lane >= 120 if d > 0 else lane < 8
    return jnp.where(end, 0.0, roll(q, -8 * d, 1))


def rim_own(q):
    return jnp.where(lanes((8, 128)) % 8 < 4, q[56:64], q[32:40])


def upwind_weights(cx, cr, cy, cd, cz, cu, dens):
    ig = 1.0 / dens
    pos, neg = (lambda a: jnp.maximum(a, 0.0)), (lambda a: jnp.minimum(a, 0.0))
    rp, rn, lp, ln = pos(cr), neg(cr), pos(cx), neg(cx)
    dp, dn, up, un = pos(cd), neg(cd), pos(cy), neg(cy)
    ap, an, bp, bn = pos(cu), neg(cu), pos(cz), neg(cz)
    mid = 1.0 - ig * (((rp - ln) + (dp - un)) + (ap - bn))
    return mid, tuple(ig * a for a in (lp, -rn, up, -dn, bp, -an)), ig


def face(c, one, two):
    return 0.5 * (jnp.abs(c) - c * c / (0.5 * (one + two)))


def anti_weights(faces, ig):
    kl, kr, ku, kd, kb, ka = faces
    mid = 1.0 + ig * (((kl + kr) + (ku + kd)) + (ka + kb))
    return mid, tuple(-ig * a for a in faces)


def seven(mid, w, p, around):
    x = w[0] * around[0] + w[1] * around[1]
    y = w[2] * around[2] + w[3] * around[3]
    z = w[4] * around[4] + w[5] * around[5]
    return (mid * p + x) + (y + z)


def field_of(refs, f):
    mom, th, cou, den, dia, cro = refs
    if f < 3:
        return mom.at[f]
    if f == TH:
        return th
    if f == G:
        return den
    if f < 8:
        return cou.at[f - 5]
    if f < 11:
        return dia.at[f - 8]
    return cro.at[f - 11]


def strips(levels):
    nz = len(levels)
    slot = lanes(levels[0].shape) // 8
    left = right = jnp.zeros(levels[0].shape, F32)
    for k, a in enumerate(levels):
        moved = roll(a, 8 * k, 1)
        left = jnp.where(slot == k, moved, left)
        right = jnp.where(slot == (k - 1) % nz, moved, right)
    return left, roll(right, 8, 1)


def fetch_kernel(*refs):
    sources, refs, (to_chip, to_other, to_up, to_down, sem) = refs[:6], refs[6:12], refs[12:]
    copies = [pltpu.make_async_copy(a, b, sem.at[i]) for i, (a, b) in enumerate(zip(sources, refs))]
    for copy in copies:
        copy.start()
    for copy in copies:
        copy.wait()
    cou = refs[2]
    nz = refs[1].shape[0]
    row = rows((8, 128))
    first_row = (row == 0) & (lax.axis_index("gy") == 0)
    for k in range(nz):
        cou[1, k] = jnp.where(first_row, 0.0, cou[1, k])
    cou[2, 0] = jnp.zeros((8, 128), F32)
    for c, (first, n, second, m) in enumerate(COMBOS):
        one, two = field_of(refs, first), field_of(refs, second)
        for k in range(nz):
            a, b = one[k], two[k]
            to_down[c, k] = jnp.where(row < n, a, roll(b, n, 0))
            to_up[c, k] = jnp.where(row >= 8 - n, a, roll(b, -n, 0))
    for f in range(NF):
        ref = field_of(refs, f)
        left, right = strips([ref[k] for k in range(nz)])
        to_chip[f] = jnp.where(even_x(), right, left)
        to_other[f] = jnp.where(even_x(), left, right)


def even_x():
    return lax.axis_index("gx") % 2 == 0


def by_side(chip, other):
    return jnp.where(even_x(), other, chip), jnp.where(even_x(), chip, other)


def corner_kernel(from_chip, from_other, to_up, to_down):
    row = rows((8, 128))
    for side in range(2):
        for c, (first, n, second, m) in enumerate(COMBOS):
            a, b = (by_side(from_chip[f], from_other[f])[side] for f in (first, second))
            to_down[side, c] = jnp.where(row < n, a, roll(b, n, 0))
            to_up[side, c] = jnp.where(row >= 8 - n, a, roll(b, -n, 0))


def halo(f, low, high):
    gy = lax.axis_index("gy")
    outside = 1.0 if f == G else 0.0
    return (
        jnp.where(gy > 0, low, outside),
        jnp.where(gy < lax.axis_size("gy") - 1, high, outside),
    )


def masks(shape):
    gy = lax.axis_index("gy")
    has_below = gy > 0
    has_above = gy < lax.axis_size("gy") - 1
    row = rows(shape) % 24
    inside = ((row >= 8) | has_below) & ((row < 16) | has_above)
    edge = ((row == 8) & ~has_below) | ((row == 16) & ~has_above)
    return inside, edge


def core_kernel(
    mom, th, cou, den, dia, cro, to_chip, to_other, below, above,
    moved, right_side, C, near_left, near_right, S, P1, M,
):
    refs = (mom, th, cou, den, dia, cro)
    nz = den.shape[0]
    shape = (24, 128)
    for c, (first, n, second, m) in enumerate(COMBOS):
        for f, shift in ((first, 0), (second, n)):
            ref = field_of(refs, f)
            outer = []
            for k in range(nz):
                low, high = halo(f, roll(below[c, k], shift, 0), roll(above[c, k], -shift, 0))
                S[f, k + 1] = jnp.concatenate((low, ref[k], high), axis=0)
                outer.append(jnp.concatenate((low, high), axis=0))
            own_strips = by_side(to_chip[f], to_other[f])
            for out, mid, ends in zip((near_left, near_right), own_strips, strips(outer)):
                out[f] = jnp.concatenate((ends[0:8], mid, ends[8:16]), axis=0)
            pad = jnp.full(shape, 1.0 if f == G else 0.0, F32)
            S[f, 0] = pad
            S[f, nz + 1] = pad
    inside, edge = masks(shape)
    zero = jnp.zeros(shape, F32)

    def upwind(k, carry):
        cx, cy, cz, cu = S[CX, k], S[CY, k], S[CZ, k], S[CZ, k + 1]
        mid, w, ig = upwind_weights(cx, xs(cx, 1), cy, ys(cy, 1), cz, cu, S[G, k])
        for f in range(4):
            psi = S[f, k]
            around = (xs(psi, -1), xs(psi, 1), ys(psi, -1), ys(psi, 1), S[f, k - 1], S[f, k + 1])
            P1[f, k] = seven(mid, w, psi, around)
        return carry

    lax.fori_loop(1, nz + 1, upwind, 0, unroll=4)
    for f in range(4):
        P1[f, 0] = zero
        P1[f, nz + 1] = zero

    def anti(k, kb):
        dens = S[G, k]
        kl = face(S[CX, k], xs(dens, -1), dens)
        ku = face(S[CY, k], ys(dens, -1), dens)
        ka = face(S[CZ, k + 1], dens, S[G, k + 1])
        mid, w = anti_weights((kl, xs(kl, 1), ku, ys(ku, 1), kb, ka), 1.0 / dens)
        for f in range(4):
            psi = P1[f, k]
            around = (xs(psi, -1), xs(psi, 1), ys(psi, -1), ys(psi, 1), P1[f, k - 1], P1[f, k + 1])
            res = seven(mid, w, psi, around)
            if f < 3:
                M[f, k] = res
            moved[f, k - 1] = res[8:16]
        return ka

    lax.fori_loop(1, nz + 1, anti, zero, unroll=4)
    M[2, 0] = zero
    M[2, nz + 1] = zero

    def first(k, carry):
        u, v = M[0, k], M[1, k]
        rhs = 0.5 * (
            (xs(u, 1) - xs(u, -1)) + (ys(v, 1) - ys(v, -1)) + (M[2, k + 1] - M[2, k - 1])
        )
        right_side[k - 1] = jnp.where(inside, rhs, 0.0)
        a11, a22, a33 = S[A11, k], S[A22, k], S[A33, k]
        wxl = 0.5 * (xs(a11, -1) + a11)
        wyl = jnp.where(edge, 0.0, 0.5 * (ys(a22, -1) + a22))
        wzl = jnp.where(k > 1, 0.5 * (S[A33, k - 1] + a33), 0.0)
        wz = jnp.where(k < nz, 0.5 * (S[A33, k + 1] + a33), 0.0)
        wx, wy = xs(wxl, 1), ys(wyl, 1)
        for n, w in enumerate((wx, wxl, wy, wyl, wz, wzl)):
            C[n, k - 1] = w
        C[6, k - 1] = ((wx + wxl) + (wy + wyl)) + ((wz + wzl) + helm)
        C[7, k - 1] = 0.25 * S[A12, k]
        C[8, k - 1] = 0.25 * S[A13, k]
        C[9, k - 1] = 0.25 * S[A23, k]
        return carry

    lax.fori_loop(1, nz + 1, first, 0, unroll=4)


def solve_kernel(
    right_side, C, near_left, near_right, from_chip, from_other, cbelow, cabove,
    basis, dxs, dys, rim_moved, rim_basis, rim_dxs, rim_dys, gram,
    VV, D, E, T,
):
    nz = right_side.shape[0]
    shape = (24, 128)
    zero = jnp.zeros(shape, F32)
    inside, edge = masks((96, 128))
    lane96 = lanes((96, 128))

    far = {}
    for c, (one, n, two, m) in enumerate(COMBOS):
        for f, shift in ((one, 0), (two, n)):
            far[f] = []
            for side, mine in enumerate(by_side(from_chip[f], from_other[f])):
                low, high = halo(
                    f, roll(cbelow[side, c], shift, 0), roll(cabove[side, c], -shift, 0)
                )
                far[f].append(jnp.concatenate((low, mine, high), axis=0))

    def rim_field(f):
        return jnp.concatenate((far[f][0], near_right[f], near_left[f], far[f][1]), axis=0)

    def around(q):
        return (
            rim_x(q, -1), rim_x(q, 1), ys(q, -1), ys(q, 1), rim_z(q, -1), rim_z(q, 1)
        )

    cx, cy, cz, dens = rim_field(CX), rim_field(CY), rim_field(CZ), rim_field(G)
    cu = rim_z(cz, 1)
    mid, w, ig = upwind_weights(cx, rim_x(cx, 1), cy, ys(cy, 1), cz, cu, dens)
    kl = face(cx, rim_x(dens, -1), dens)
    ku = face(cy, ys(dens, -1), dens)
    kb = face(cz, roll(dens, 8, 1), dens)
    mid2, w2 = anti_weights((kl, rim_x(kl, 1), ku, ys(ku, 1), kb, rim_z(kb, 1)), ig)
    done = []
    for f in range(4):
        psi = rim_field(f)
        psi = seven(mid, w, psi, around(psi))
        psi = seven(mid2, w2, psi, around(psi))
        rim_moved[f] = rim_own(psi)
        done.append(psi)
    u, v, t = done[:3]
    v0 = 0.5 * (
        (rim_x(u, 1) - rim_x(u, -1)) + (ys(v, 1) - ys(v, -1)) + (rim_z(t, 1) - rim_z(t, -1))
    )
    v0 = jnp.where(inside, v0, 0.0)

    lane = lanes(shape)
    c24 = lane % 8
    slot = lane // 8
    edges = jnp.where(c24 < 4, v0[48:72], v0[24:48])
    turned = [roll(edges, -8 * k, 1) for k in range(nz)]
    inner = zero
    for k in range(nz):
        core = right_side[k]
        VV[0, k + 1] = jnp.where(
            lane < 4, turned[k], jnp.where(lane >= 124, turned[(k + 1) % nz], core)
        )
        take = ((slot == k) & (c24 >= 4)) | ((slot == (k - 1) % nz) & (c24 < 4))
        inner = jnp.where(take, roll(core, 8 * k, 1), inner)
    q = jnp.concatenate(
        (
            v0[0:24],
            jnp.where(c24 < 4, roll(inner, 8, 1), v0[24:48]),
            jnp.where(c24 >= 4, inner, v0[48:72]),
            v0[72:96],
        ),
        axis=0,
    )

    a11, a22, a33 = rim_field(A11), rim_field(A22), rim_field(A33)
    wxl = 0.5 * (rim_x(a11, -1) + a11)
    wyl = jnp.where(edge, 0.0, 0.5 * (ys(a22, -1) + a22))
    wzl = jnp.where(lane96 < 8, 0.0, 0.5 * (roll(a33, 8, 1) + a33))
    wx, wy, wz = rim_x(wxl, 1), ys(wyl, 1), rim_z(wzl, 1)
    wc = ((wx + wxl) + (wy + wyl)) + ((wz + wzl) + helm)
    q12, q13, q23 = (0.25 * rim_field(f) for f in (A12, A13, A23))
    rims = [rim_own(q)]
    rim_basis[0] = rims[0]
    for i in range(3):
        xm, xp, ym, yp, zm, zp = around(q)
        d, e = xp - xm, yp - ym
        rim_dxs[i] = rim_own(d)
        rim_dys[i] = rim_own(e)
        new = seven(-wc, (wxl, wx, wyl, wy, wzl, wz), q, (xm, xp, ym, yp, zm, zp))
        new = new + q12 * (ys(d, 1) - ys(d, -1))
        new = new + q13 * (rim_z(d, 1) - rim_z(d, -1))
        q = new + q23 * (rim_z(e, 1) - rim_z(e, -1))
        rims.append(rim_own(q))
        if i < 2:
            rim_basis[i + 1] = rims[-1]

    for i in range(3):
        VV[i, 0] = zero
        VV[i, nz + 1] = zero
    for a in (D, E):
        a[0] = zero
        a[nz + 1] = zero
    own = lambda a: a[8:16]
    sums = {}
    for i in range(3):
        last = i == 2
        cut = own if last else (lambda a: a)

        def flat(k, carry, i=i, cut=cut, last=last):
            p = VV[i, k]
            xp, xm, yp, ym = xs(p, 1), xs(p, -1), ys(p, 1), ys(p, -1)
            d, e = xp - xm, yp - ym
            D[k] = d
            E[k] = e
            dxs[i, k - 1] = own(d)
            dys[i, k - 1] = own(e)
            basis[i, k - 1] = own(p)
            near = (xp, xm, yp, ym, VV[i, k + 1], VV[i, k - 1])
            t = seven(-cut(C[6, k - 1]), [cut(C[n, k - 1]) for n in range(6)], cut(p), [cut(a) for a in near])
            t = t + cut(C[7, k - 1]) * cut(ys(d, 1) - ys(d, -1))
            if last:
                T[k, 8:16] = t
            else:
                T[k] = t
            return carry

        lax.fori_loop(1, nz + 1, flat, 0, unroll=4)
        pairs = [(j, i + 1) for j in range(i + 2)]

        def deep(k, acc, i=i, cut=cut, last=last, pairs=pairs):
            v = cut(T[k]) + cut(C[8, k - 1]) * (cut(D[k + 1]) - cut(D[k - 1]))
            v = v + cut(C[9, k - 1]) * (cut(E[k + 1]) - cut(E[k - 1]))
            if not last:
                VV[i + 1, k] = v
                v = own(v)
            vs = [own(VV[j, k]) for j in range(i + 1)] + [v]
            return tuple(s + vs[j] * v for s, (j, _) in zip(acc, pairs))

        start = (jnp.zeros((8, 128), F32),) * len(pairs)
        acc = lax.fori_loop(1, nz + 1, deep, start, unroll=4)
        for s, key in zip(acc, pairs):
            sums[key] = s
    lane8 = lanes((8, 128))
    core_part = (lane8 >= 4) & (lane8 < 124)
    line = lanes((1, 128))
    out = jnp.zeros((1, 128), F32)
    for n, (i, j) in enumerate(KEYS):
        s = jnp.where(core_part, sums[(i, j)], 0.0) + rims[i] * rims[j]
        s = jnp.sum(jnp.sum(s, axis=0, keepdims=True), axis=1, keepdims=True)
        out = jnp.where(line == n, s, out)
    gram[...] = jnp.broadcast_to(out, gram.shape)


KEYS = ((0, 1), (1, 1), (0, 2), (1, 2), (2, 2), (0, 3), (1, 3), (2, 3), (3, 3))


def weights(gram):
    def inner(a, b):
        total = 0.0
        for i in range(4):
            for j in range(4):
                if a[i] is not None and b[j] is not None:
                    total = total + a[i] * b[j] * gram[(min(i, j), max(i, j))]
        return total

    def less(a, s, b):
        out = []
        for one, two in zip(a, b):
            if two is None:
                out.append(one)
            else:
                out.append(-(s * two) if one is None else one - s * two)
        return out

    one = jnp.ones((1, 1), F32)
    r = [one, None, None, None]
    sol = [None] * 4
    dirs, images, norms = [r], [[None, one, None, None]], []
    for n in range(ITERS):
        norms.append(inner(images[n], images[n]))
        beta = inner(r, images[n]) / norms[n]
        sol = less(sol, -beta, dirs[n])
        r = less(r, beta, images[n])
        if n + 1 < ITERS:
            z = [None] + r[:3]
            new_dir, new_img = r, z
            for l in range(n + 1):
                alpha = inner(z, images[l]) / norms[l]
                new_dir = less(new_dir, alpha, dirs[l])
                new_img = less(new_img, alpha, images[l])
            dirs.append(new_dir)
            images.append(new_img)
    return sol[:3]


def last_kernel(
    partial, moved, basis, dxs, dys, rim_moved, rim_basis, rim_dxs, rim_dys,
    momenta_out, theta_out, pressure,
):
    nz = moved.shape[1]
    total = jnp.sum(partial[...], axis=0, keepdims=True)
    line = lanes(total.shape)
    gram = {
        key: jnp.sum(jnp.where(line == n, total, 0.0), axis=1, keepdims=True)
        for n, key in enumerate(KEYS)
    }
    c = [jnp.broadcast_to(s, (8, 128)) for s in weights(gram)]
    h = [0.5 * s for s in c]
    lane = lanes((8, 128))

    def mix(s, a):
        return (s[0] * a[0] + s[1] * a[1]) + s[2] * a[2]

    def joined(rim, core):
        turned = [roll(rim, -8 * k, 1) for k in range(nz)]
        return [
            jnp.where(lane < 4, turned[k], jnp.where(lane >= 124, turned[(k + 1) % nz], core[k]))
            for k in range(nz)
        ]

    p_rim = mix(c, rim_basis)
    p = joined(p_rim, [mix(c, [basis[i, k] for i in range(3)]) for k in range(nz)])
    for k in range(nz):
        pressure[k] = p[k]
    zero = jnp.zeros((8, 128), F32)
    for n, (diff, rim_diff) in enumerate(((dxs, rim_dxs), (dys, rim_dys))):
        core = [moved[n, k] - mix(h, [diff[i, k] for i in range(3)]) for k in range(nz)]
        for k, a in enumerate(joined(rim_moved[n] - mix(h, rim_diff), core)):
            momenta_out[n, k] = a
    for k, a in enumerate(joined(rim_moved[2], [moved[2, k] for k in range(nz)])):
        above = p[k + 1] if k + 1 < nz else zero
        below = p[k - 1] if k > 0 else zero
        momenta_out[2, k] = a - 0.5 * (above - below)
    for k, a in enumerate(joined(rim_moved[3], [moved[3, k] for k in range(nz)])):
        theta_out[k] = a


def shift_to(a, axis, step):
    n = lax.axis_size(axis)
    return lax.ppermute(a, axis, [(i, (i + step) % n) for i in range(n)])


def swap(a, axis, start):
    n = lax.axis_size(axis)
    pairs = []
    for i in range(start, n + start, 2):
        pairs += [(i % n, (i + 1) % n), ((i + 1) % n, i % n)]
    return lax.ppermute(a, axis, pairs)


def call(kernel, name, out, scratch=(), space=pltpu.VMEM, limit=16, cost=None):
    def run(*args):
        return pl.pallas_call(
            kernel,
            out_shape=tuple(jax.ShapeDtypeStruct(a, F32) for a in out),
            in_specs=[pl.BlockSpec(memory_space=space)] * len(args),
            out_specs=[pl.BlockSpec(memory_space=pltpu.VMEM)] * len(out),
            scratch_shapes=list(scratch),
            compiler_params=pltpu.CompilerParams(vmem_limit_bytes=limit << 20),
            cost_estimate=cost,
            name=name,
        )(*args)

    return run


def local(momenta, theta, courant, density, metric_diag, metric_cross):
    nz = density.shape[0]
    args = (momenta, theta, courant, density, metric_diag, metric_cross)
    block = (nz, 8, 128)
    core = (nz, 24, 128)
    deep = (nz + 2, 24, 128)
    nx, ny = lax.axis_size("gx"), lax.axis_size("gy")
    rows_out = (len(COMBOS), nz, 8, 128)

    tiles = (NF, 8, 128)
    *args, to_chip, to_other, to_up, to_down = call(
        fetch_kernel,
        "fetch",
        [a.shape for a in args] + [tiles] * 2 + [rows_out] * 2,
        [pltpu.SemaphoreType.DMA((6,))],
        pltpu.HBM,
    )(*(pltpu.with_memory_space_constraint(a, pltpu.HBM) for a in args))
    below = shift_to(to_up, "gy", 1)
    above = shift_to(to_down, "gy", -1)
    from_other = swap(to_other, "gx", 1)
    from_chip = swap(to_chip, "gx", 0)
    corner_up, corner_down = call(
        corner_kernel,
        "corner",
        [(2, len(COMBOS), 8, 128)] * 2,
        cost=pl.CostEstimate(flops=10**10, transcendentals=0, bytes_accessed=10**9),
    )(from_chip, from_other)
    cbelow = shift_to(corner_up, "gy", 1)
    cabove = shift_to(corner_down, "gy", -1)
    moved, right_side, coef, near_left, near_right = call(
        core_kernel,
        "core",
        [(4,) + block, core, (10,) + core] + [(NF, 24, 128)] * 2,
        [pltpu.VMEM((n,) + deep, F32) for n in (NF, 4, 3)],
    )(*args, to_chip, to_other, below, above)
    three, rim = (3,) + block, (3, 8, 128)
    *parts, gram = call(
        solve_kernel,
        "solve",
        [three] * 3 + [(4, 8, 128), rim, rim, rim, (nx, 128)],
        [pltpu.VMEM((3,) + deep, F32)] + [pltpu.VMEM(deep, F32)] * 3,
    )(right_side, coef, near_left, near_right, from_chip, from_other, cbelow, cabove)

    part = lax.all_to_all(gram, "gx", 0, 0, tiled=True)
    part = jnp.broadcast_to(jnp.sum(part, axis=0, keepdims=True), (ny, 128))
    part = lax.all_to_all(part, "gy", 0, 0, tiled=True)
    momenta_out, theta_out, pressure = call(
        last_kernel, "combine", [three, block, block]
    )(part, moved, *parts)
    return (momenta_out, theta_out, pressure)


def solution(mesh):
    placed = (
        P(None, None, "gy", "gx"),
        P(None, "gy", "gx"),
        P(None, None, "gy", "gx"),
        P(None, "gy", "gx"),
        P(None, None, "gy", "gx"),
        P(None, None, "gy", "gx"),
    )
    return jax.shard_map(
        local,
        mesh=mesh,
        in_specs=placed,
        out_specs=(P(None, None, "gy", "gx"), P(None, "gy", "gx"), P(None, "gy", "gx")),
        check_vma=False,
    )
```

```python
import jax
import jax.numpy as jnp
from jax import lax
from jax.experimental import pallas as pl
from jax.experimental.pallas import tpu as pltpu
from jax.sharding import PartitionSpec as P

helm = 0.02
ITERS = 3
NF = 14
U, V, W, TH, G, CX, CY, CZ, A11, A22, A33, A12, A13, A23 = range(NF)
COMBOS = (
    (V, 6, TH, 2),
    (CY, 6, A12, 2),
    (U, 5, A22, 3),
    (W, 5, A11, 2),
    (G, 5, A33, 2),
    (CX, 5, A13, 2),
    (CZ, 5, A23, 2),
)
F32 = jnp.float32


def lanes(shape):
    return lax.broadcasted_iota(jnp.int32, shape, len(shape) - 1)


def rows(shape):
    return lax.broadcasted_iota(jnp.int32, shape, len(shape) - 2)


def roll(a, shift, axis):
    shift = shift % a.shape[axis]
    if shift == 0:
        return a
    return pltpu.roll(a, shift, axis)


def xs(a, d):
    return roll(a, -d, 1)


def ys(a, d):
    return roll(a, -d, 0)


def rim_x(q, d):
    c = lanes((48, 128)) % 8
    moved = roll(q, -d, 1)
    if d > 0:
        first = jnp.where(c == 7, roll(q[48:], 7, 1), moved[:48])
        return jnp.concatenate((first, moved[48:]), axis=0)
    last = jnp.where(c == 0, roll(q[:48], -7, 1), moved[48:])
    return jnp.concatenate((moved[:48], last), axis=0)


def rim_z(q, d):
    lane = lanes(q.shape)
    end = lane >= 120 if d > 0 else lane < 8
    return jnp.where(end, 0.0, roll(q, -8 * d, 1))


def rim_own(q):
    return jnp.where(lanes((8, 128)) % 8 < 4, q[56:64], q[32:40])


def upwind_weights(cx, cr, cy, cd, cz, cu, dens):
    ig = 1.0 / dens
    pos, neg = (lambda a: jnp.maximum(a, 0.0)), (lambda a: jnp.minimum(a, 0.0))
    rp, rn, lp, ln = pos(cr), neg(cr), pos(cx), neg(cx)
    dp, dn, up, un = pos(cd), neg(cd), pos(cy), neg(cy)
    ap, an, bp, bn = pos(cu), neg(cu), pos(cz), neg(cz)
    mid = 1.0 - ig * (((rp - ln) + (dp - un)) + (ap - bn))
    return mid, tuple(ig * a for a in (lp, -rn, up, -dn, bp, -an)), ig


def face(c, one, two):
    return 0.5 * (jnp.abs(c) - c * c / (0.5 * (one + two)))


def anti_weights(faces, ig):
    kl, kr, ku, kd, kb, ka = faces
    mid = 1.0 + ig * (((kl + kr) + (ku + kd)) + (ka + kb))
    return mid, tuple(-ig * a for a in faces)


def seven(mid, w, p, around):
    x = w[0] * around[0] + w[1] * around[1]
    y = w[2] * around[2] + w[3] * around[3]
    z = w[4] * around[4] + w[5] * around[5]
    return (mid * p + x) + (y + z)


def field_of(refs, f):
    mom, th, cou, den, dia, cro = refs
    if f < 3:
        return mom.at[f]
    if f == TH:
        return th
    if f == G:
        return den
    if f < 8:
        return cou.at[f - 5]
    if f < 11:
        return dia.at[f - 8]
    return cro.at[f - 11]


def strips(levels):
    nz = len(levels)
    slot = lanes(levels[0].shape) // 8
    left = right = jnp.zeros(levels[0].shape, F32)
    for k, a in enumerate(levels):
        moved = roll(a, 8 * k, 1)
        left = jnp.where(slot == k, moved, left)
        right = jnp.where(slot == (k - 1) % nz, moved, right)
    return left, roll(right, 8, 1)


def fetch_kernel(*refs):
    sources, refs, (to_chip, to_other, to_up, to_down, sem) = refs[:6], refs[6:12], refs[12:]
    copies = [pltpu.make_async_copy(a, b, sem.at[i]) for i, (a, b) in enumerate(zip(sources, refs))]
    for copy in copies:
        copy.start()
    for copy in copies:
        copy.wait()
    cou = refs[2]
    nz = refs[1].shape[0]
    row = rows((8, 128))
    first_row = (row == 0) & (lax.axis_index("gy") == 0)
    for k in range(nz):
        cou[1, k] = jnp.where(first_row, 0.0, cou[1, k])
    cou[2, 0] = jnp.zeros((8, 128), F32)
    for c, (first, n, second, m) in enumerate(COMBOS):
        one, two = field_of(refs, first), field_of(refs, second)
        for k in range(nz):
            a, b = one[k], two[k]
            to_down[c, k] = jnp.where(row < n, a, roll(b, n, 0))
            to_up[c, k] = jnp.where(row >= 8 - n, a, roll(b, -n, 0))
    for f in range(NF):
        ref = field_of(refs, f)
        left, right = strips([ref[k] for k in range(nz)])
        to_chip[f] = jnp.where(even_x(), right, left)
        to_other[f] = jnp.where(even_x(), left, right)


def even_x():
    return lax.axis_index("gx") % 2 == 0


def by_side(chip, other):
    return jnp.where(even_x(), other, chip), jnp.where(even_x(), chip, other)


def corner_tiles(strip):
    row = rows((8, 128))
    for c, (first, n, second, m) in enumerate(COMBOS):
        a, b = strip[first], strip[second]
        up = jnp.where(row >= 8 - n, a, roll(b, -n, 0))
        yield c, up, jnp.where(row < n, a, roll(b, n, 0))


def other_kernel(from_other, to_up, to_down):
    for c, up, down in corner_tiles(from_other):
        to_up[c] = up
        to_down[c] = down


def chip_kernel(from_chip, other_up, other_down, to_up, to_down):
    to_up[0] = other_up[...]
    to_down[0] = other_down[...]
    for c, up, down in corner_tiles(from_chip):
        to_up[1, c] = up
        to_down[1, c] = down


def halo(f, low, high):
    gy = lax.axis_index("gy")
    outside = 1.0 if f == G else 0.0
    return (
        jnp.where(gy > 0, low, outside),
        jnp.where(gy < lax.axis_size("gy") - 1, high, outside),
    )


def masks(shape):
    gy = lax.axis_index("gy")
    has_below = gy > 0
    has_above = gy < lax.axis_size("gy") - 1
    row = rows(shape) % 24
    inside = ((row >= 8) | has_below) & ((row < 16) | has_above)
    edge = ((row == 8) & ~has_below) | ((row == 16) & ~has_above)
    return inside, edge


def core_kernel(
    mom, th, cou, den, dia, cro, to_chip, to_other, below, above,
    moved, right_side, C, near_left, near_right, S, P1, M,
):
    refs = (mom, th, cou, den, dia, cro)
    nz = den.shape[0]
    shape = (24, 128)
    for c, (first, n, second, m) in enumerate(COMBOS):
        for f, shift in ((first, 0), (second, n)):
            ref = field_of(refs, f)
            outer = []
            for k in range(nz):
                low, high = halo(f, roll(below[c, k], shift, 0), roll(above[c, k], -shift, 0))
                S[f, k + 1] = jnp.concatenate((low, ref[k], high), axis=0)
                outer.append(jnp.concatenate((low, high), axis=0))
            own_strips = by_side(to_chip[f], to_other[f])
            for out, mid, ends in zip((near_left, near_right), own_strips, strips(outer)):
                out[f] = jnp.concatenate((ends[0:8], mid, ends[8:16]), axis=0)
            pad = jnp.full(shape, 1.0 if f == G else 0.0, F32)
            S[f, 0] = pad
            S[f, nz + 1] = pad
    inside, edge = masks(shape)
    zero = jnp.zeros(shape, F32)

    def upwind(k, carry):
        cx, cy, cz, cu = S[CX, k], S[CY, k], S[CZ, k], S[CZ, k + 1]
        mid, w, ig = upwind_weights(cx, xs(cx, 1), cy, ys(cy, 1), cz, cu, S[G, k])
        for f in range(4):
            psi = S[f, k]
            around = (xs(psi, -1), xs(psi, 1), ys(psi, -1), ys(psi, 1), S[f, k - 1], S[f, k + 1])
            P1[f, k] = seven(mid, w, psi, around)
        return carry

    lax.fori_loop(1, nz + 1, upwind, 0, unroll=4)
    for f in range(4):
        P1[f, 0] = zero
        P1[f, nz + 1] = zero

    def anti(k, kb):
        dens = S[G, k]
        kl = face(S[CX, k], xs(dens, -1), dens)
        ku = face(S[CY, k], ys(dens, -1), dens)
        ka = face(S[CZ, k + 1], dens, S[G, k + 1])
        mid, w = anti_weights((kl, xs(kl, 1), ku, ys(ku, 1), kb, ka), 1.0 / dens)
        for f in range(4):
            psi = P1[f, k]
            around = (xs(psi, -1), xs(psi, 1), ys(psi, -1), ys(psi, 1), P1[f, k - 1], P1[f, k + 1])
            res = seven(mid, w, psi, around)
            if f < 3:
                M[f, k] = res
            moved[f, k - 1] = res[8:16]
        return ka

    lax.fori_loop(1, nz + 1, anti, zero, unroll=4)
    M[2, 0] = zero
    M[2, nz + 1] = zero

    def first(k, carry):
        u, v = M[0, k], M[1, k]
        rhs = 0.5 * (
            (xs(u, 1) - xs(u, -1)) + (ys(v, 1) - ys(v, -1)) + (M[2, k + 1] - M[2, k - 1])
        )
        right_side[k - 1] = jnp.where(inside, rhs, 0.0)
        a11, a22, a33 = S[A11, k], S[A22, k], S[A33, k]
        wxl = 0.5 * (xs(a11, -1) + a11)
        wyl = jnp.where(edge, 0.0, 0.5 * (ys(a22, -1) + a22))
        wzl = jnp.where(k > 1, 0.5 * (S[A33, k - 1] + a33), 0.0)
        wz = jnp.where(k < nz, 0.5 * (S[A33, k + 1] + a33), 0.0)
        wx, wy = xs(wxl, 1), ys(wyl, 1)
        for n, w in enumerate((wx, wxl, wy, wyl, wz, wzl)):
            C[n, k - 1] = w
        C[6, k - 1] = ((wx + wxl) + (wy + wyl)) + ((wz + wzl) + helm)
        C[7, k - 1] = 0.25 * S[A12, k]
        C[8, k - 1] = 0.25 * S[A13, k]
        C[9, k - 1] = 0.25 * S[A23, k]
        return carry

    lax.fori_loop(1, nz + 1, first, 0, unroll=4)


def solve_kernel(
    right_side, C, near_left, near_right, from_chip, from_other, cbelow, cabove,
    basis, dxs, dys, rim_moved, rim_basis, rim_dxs, rim_dys, gram,
    VV, D, E, T,
):
    nz = right_side.shape[0]
    shape = (24, 128)
    zero = jnp.zeros(shape, F32)
    inside, edge = masks((96, 128))
    lane96 = lanes((96, 128))

    far = {}
    for c, (one, n, two, m) in enumerate(COMBOS):
        for f, shift in ((one, 0), (two, n)):
            far[f] = []
            lows = by_side(cbelow[1, c], cbelow[0, c])
            highs = by_side(cabove[1, c], cabove[0, c])
            for side, mine in enumerate(by_side(from_chip[f], from_other[f])):
                low, high = halo(f, roll(lows[side], shift, 0), roll(highs[side], -shift, 0))
                far[f].append(jnp.concatenate((low, mine, high), axis=0))

    def rim_field(f):
        return jnp.concatenate((far[f][0], near_right[f], near_left[f], far[f][1]), axis=0)

    def around(q):
        return (
            rim_x(q, -1), rim_x(q, 1), ys(q, -1), ys(q, 1), rim_z(q, -1), rim_z(q, 1)
        )

    cx, cy, cz, dens = rim_field(CX), rim_field(CY), rim_field(CZ), rim_field(G)
    cu = rim_z(cz, 1)
    mid, w, ig = upwind_weights(cx, rim_x(cx, 1), cy, ys(cy, 1), cz, cu, dens)
    kl = face(cx, rim_x(dens, -1), dens)
    ku = face(cy, ys(dens, -1), dens)
    kb = face(cz, roll(dens, 8, 1), dens)
    mid2, w2 = anti_weights((kl, rim_x(kl, 1), ku, ys(ku, 1), kb, rim_z(kb, 1)), ig)
    done = []
    for f in range(4):
        psi = rim_field(f)
        psi = seven(mid, w, psi, around(psi))
        psi = seven(mid2, w2, psi, around(psi))
        rim_moved[f] = rim_own(psi)
        done.append(psi)
    u, v, t = done[:3]
    v0 = 0.5 * (
        (rim_x(u, 1) - rim_x(u, -1)) + (ys(v, 1) - ys(v, -1)) + (rim_z(t, 1) - rim_z(t, -1))
    )
    v0 = jnp.where(inside, v0, 0.0)

    lane = lanes(shape)
    c24 = lane % 8
    slot = lane // 8
    edges = jnp.where(c24 < 4, v0[48:72], v0[24:48])
    turned = [roll(edges, -8 * k, 1) for k in range(nz)]
    inner = zero
    for k in range(nz):
        core = right_side[k]
        VV[0, k + 1] = jnp.where(
            lane < 4, turned[k], jnp.where(lane >= 124, turned[(k + 1) % nz], core)
        )
        take = ((slot == k) & (c24 >= 4)) | ((slot == (k - 1) % nz) & (c24 < 4))
        inner = jnp.where(take, roll(core, 8 * k, 1), inner)
    q = jnp.concatenate(
        (
            v0[0:24],
            jnp.where(c24 < 4, roll(inner, 8, 1), v0[24:48]),
            jnp.where(c24 >= 4, inner, v0[48:72]),
            v0[72:96],
        ),
        axis=0,
    )

    a11, a22, a33 = rim_field(A11), rim_field(A22), rim_field(A33)
    wxl = 0.5 * (rim_x(a11, -1) + a11)
    wyl = jnp.where(edge, 0.0, 0.5 * (ys(a22, -1) + a22))
    wzl = jnp.where(lane96 < 8, 0.0, 0.5 * (roll(a33, 8, 1) + a33))
    wx, wy, wz = rim_x(wxl, 1), ys(wyl, 1), rim_z(wzl, 1)
    wc = ((wx + wxl) + (wy + wyl)) + ((wz + wzl) + helm)
    q12, q13, q23 = (0.25 * rim_field(f) for f in (A12, A13, A23))
    rims = [rim_own(q)]
    rim_basis[0] = rims[0]
    for i in range(3):
        xm, xp, ym, yp, zm, zp = around(q)
        d, e = xp - xm, yp - ym
        rim_dxs[i] = rim_own(d)
        rim_dys[i] = rim_own(e)
        new = seven(-wc, (wxl, wx, wyl, wy, wzl, wz), q, (xm, xp, ym, yp, zm, zp))
        new = new + q12 * (ys(d, 1) - ys(d, -1))
        new = new + q13 * (rim_z(d, 1) - rim_z(d, -1))
        q = new + q23 * (rim_z(e, 1) - rim_z(e, -1))
        rims.append(rim_own(q))
        if i < 2:
            rim_basis[i + 1] = rims[-1]

    for i in range(3):
        VV[i, 0] = zero
        VV[i, nz + 1] = zero
    for a in (D, E):
        a[0] = zero
        a[nz + 1] = zero
    own = lambda a: a[8:16]
    sums = {}
    for i in range(3):
        last = i == 2
        cut = own if last else (lambda a: a)

        def flat(k, carry, i=i, cut=cut, last=last):
            p = VV[i, k]
            xp, xm, yp, ym = xs(p, 1), xs(p, -1), ys(p, 1), ys(p, -1)
            d, e = xp - xm, yp - ym
            D[k] = d
            E[k] = e
            dxs[i, k - 1] = own(d)
            dys[i, k - 1] = own(e)
            basis[i, k - 1] = own(p)
            near = (xp, xm, yp, ym, VV[i, k + 1], VV[i, k - 1])
            t = seven(-cut(C[6, k - 1]), [cut(C[n, k - 1]) for n in range(6)], cut(p), [cut(a) for a in near])
            t = t + cut(C[7, k - 1]) * cut(ys(d, 1) - ys(d, -1))
            if last:
                T[k, 8:16] = t
            else:
                T[k] = t
            return carry

        lax.fori_loop(1, nz + 1, flat, 0, unroll=4)
        pairs = [(j, i + 1) for j in range(i + 2)]

        def deep(k, acc, i=i, cut=cut, last=last, pairs=pairs):
            v = cut(T[k]) + cut(C[8, k - 1]) * (cut(D[k + 1]) - cut(D[k - 1]))
            v = v + cut(C[9, k - 1]) * (cut(E[k + 1]) - cut(E[k - 1]))
            if not last:
                VV[i + 1, k] = v
                v = own(v)
            vs = [own(VV[j, k]) for j in range(i + 1)] + [v]
            return tuple(s + vs[j] * v for s, (j, _) in zip(acc, pairs))

        start = (jnp.zeros((8, 128), F32),) * len(pairs)
        acc = lax.fori_loop(1, nz + 1, deep, start, unroll=4)
        for s, key in zip(acc, pairs):
            sums[key] = s
    lane8 = lanes((8, 128))
    core_part = (lane8 >= 4) & (lane8 < 124)
    line = lanes((1, 128))
    out = jnp.zeros((1, 128), F32)
    for n, (i, j) in enumerate(KEYS):
        s = jnp.where(core_part, sums[(i, j)], 0.0) + rims[i] * rims[j]
        s = jnp.sum(jnp.sum(s, axis=0, keepdims=True), axis=1, keepdims=True)
        out = jnp.where(line == n, s, out)
    gram[...] = jnp.broadcast_to(out, gram.shape)


KEYS = ((0, 1), (1, 1), (0, 2), (1, 2), (2, 2), (0, 3), (1, 3), (2, 3), (3, 3))


def weights(gram):
    def inner(a, b):
        total = 0.0
        for i in range(4):
            for j in range(4):
                if a[i] is not None and b[j] is not None:
                    total = total + a[i] * b[j] * gram[(min(i, j), max(i, j))]
        return total

    def less(a, s, b):
        out = []
        for one, two in zip(a, b):
            if two is None:
                out.append(one)
            else:
                out.append(-(s * two) if one is None else one - s * two)
        return out

    one = jnp.ones((1, 1), F32)
    r = [one, None, None, None]
    sol = [None] * 4
    dirs, images, norms = [r], [[None, one, None, None]], []
    for n in range(ITERS):
        norms.append(inner(images[n], images[n]))
        beta = inner(r, images[n]) / norms[n]
        sol = less(sol, -beta, dirs[n])
        r = less(r, beta, images[n])
        if n + 1 < ITERS:
            z = [None] + r[:3]
            new_dir, new_img = r, z
            for l in range(n + 1):
                alpha = inner(z, images[l]) / norms[l]
                new_dir = less(new_dir, alpha, dirs[l])
                new_img = less(new_img, alpha, images[l])
            dirs.append(new_dir)
            images.append(new_img)
    return sol[:3]


def last_kernel(
    partial, moved, basis, dxs, dys, rim_moved, rim_basis, rim_dxs, rim_dys,
    momenta_out, theta_out, pressure,
):
    nz = moved.shape[1]
    total = jnp.sum(partial[...], axis=0, keepdims=True)
    line = lanes(total.shape)
    gram = {
        key: jnp.sum(jnp.where(line == n, total, 0.0), axis=1, keepdims=True)
        for n, key in enumerate(KEYS)
    }
    c = [jnp.broadcast_to(s, (8, 128)) for s in weights(gram)]
    h = [0.5 * s for s in c]
    lane = lanes((8, 128))

    def mix(s, a):
        return (s[0] * a[0] + s[1] * a[1]) + s[2] * a[2]

    def joined(rim, core):
        turned = [roll(rim, -8 * k, 1) for k in range(nz)]
        return [
            jnp.where(lane < 4, turned[k], jnp.where(lane >= 124, turned[(k + 1) % nz], core[k]))
            for k in range(nz)
        ]

    p_rim = mix(c, rim_basis)
    p = joined(p_rim, [mix(c, [basis[i, k] for i in range(3)]) for k in range(nz)])
    for k in range(nz):
        pressure[k] = p[k]
    zero = jnp.zeros((8, 128), F32)
    for n, (diff, rim_diff) in enumerate(((dxs, rim_dxs), (dys, rim_dys))):
        core = [moved[n, k] - mix(h, [diff[i, k] for i in range(3)]) for k in range(nz)]
        for k, a in enumerate(joined(rim_moved[n] - mix(h, rim_diff), core)):
            momenta_out[n, k] = a
    for k, a in enumerate(joined(rim_moved[2], [moved[2, k] for k in range(nz)])):
        above = p[k + 1] if k + 1 < nz else zero
        below = p[k - 1] if k > 0 else zero
        momenta_out[2, k] = a - 0.5 * (above - below)
    for k, a in enumerate(joined(rim_moved[3], [moved[3, k] for k in range(nz)])):
        theta_out[k] = a


def shift_to(a, axis, step):
    n = lax.axis_size(axis)
    return lax.ppermute(a, axis, [(i, (i + step) % n) for i in range(n)])


def swap(a, axis, start):
    n = lax.axis_size(axis)
    pairs = []
    for i in range(start, n + start, 2):
        pairs += [(i % n, (i + 1) % n), ((i + 1) % n, i % n)]
    return lax.ppermute(a, axis, pairs)


def call(kernel, name, out, scratch=(), space=pltpu.VMEM, limit=16, cost=None):
    def run(*args):
        return pl.pallas_call(
            kernel,
            out_shape=tuple(jax.ShapeDtypeStruct(a, F32) for a in out),
            in_specs=[pl.BlockSpec(memory_space=space)] * len(args),
            out_specs=[pl.BlockSpec(memory_space=pltpu.VMEM)] * len(out),
            scratch_shapes=list(scratch),
            compiler_params=pltpu.CompilerParams(vmem_limit_bytes=limit << 20),
            cost_estimate=cost,
            name=name,
        )(*args)

    return run


def local(momenta, theta, courant, density, metric_diag, metric_cross):
    nz = density.shape[0]
    args = (momenta, theta, courant, density, metric_diag, metric_cross)
    block = (nz, 8, 128)
    core = (nz, 24, 128)
    deep = (nz + 2, 24, 128)
    nx, ny = lax.axis_size("gx"), lax.axis_size("gy")
    rows_out = (len(COMBOS), nz, 8, 128)

    tiles = (NF, 8, 128)
    *args, to_chip, to_other, to_up, to_down = call(
        fetch_kernel,
        "fetch",
        [a.shape for a in args] + [tiles] * 2 + [rows_out] * 2,
        [pltpu.SemaphoreType.DMA((6,))],
        pltpu.HBM,
    )(*(pltpu.with_memory_space_constraint(a, pltpu.HBM) for a in args))
    below = shift_to(to_up, "gy", 1)
    above = shift_to(to_down, "gy", -1)
    from_other = swap(to_other, "gx", 1)
    from_chip = swap(to_chip, "gx", 0)
    pair = (len(COMBOS), 8, 128)
    other_up, other_down = call(
        other_kernel,
        "other",
        [pair] * 2,
        cost=pl.CostEstimate(flops=10**10, transcendentals=0, bytes_accessed=10**9),
    )(from_other)
    corner_up, corner_down = call(chip_kernel, "chip", [(2,) + pair] * 2)(
        from_chip, other_up, other_down
    )
    cbelow = shift_to(corner_up, "gy", 1)
    cabove = shift_to(corner_down, "gy", -1)
    moved, right_side, coef, near_left, near_right = call(
        core_kernel,
        "core",
        [(4,) + block, core, (10,) + core] + [(NF, 24, 128)] * 2,
        [pltpu.VMEM((n,) + deep, F32) for n in (NF, 4, 3)],
    )(*args, to_chip, to_other, below, above)
    three, rim = (3,) + block, (3, 8, 128)
    *parts, gram = call(
        solve_kernel,
        "solve",
        [three] * 3 + [(4, 8, 128), rim, rim, rim, (nx, 128)],
        [pltpu.VMEM((3,) + deep, F32)] + [pltpu.VMEM(deep, F32)] * 3,
    )(right_side, coef, near_left, near_right, from_chip, from_other, cbelow, cabove)

    part = lax.all_to_all(gram, "gx", 0, 0, tiled=True)
    part = jnp.broadcast_to(jnp.sum(part, axis=0, keepdims=True), (ny, 128))
    part = lax.all_to_all(part, "gy", 0, 0, tiled=True)
    momenta_out, theta_out, pressure = call(
        last_kernel, "combine", [three, block, block]
    )(part, moved, *parts)
    return (momenta_out, theta_out, pressure)


def solution(mesh):
    placed = (
        P(None, None, "gy", "gx"),
        P(None, "gy", "gx"),
        P(None, None, "gy", "gx"),
        P(None, "gy", "gx"),
        P(None, None, "gy", "gx"),
        P(None, None, "gy", "gx"),
    )
    return jax.shard_map(
        local,
        mesh=mesh,
        in_specs=placed,
        out_specs=(P(None, None, "gy", "gx"), P(None, "gy", "gx"), P(None, "gy", "gx")),
        check_vma=False,
    )
```

```python
import jax
import jax.numpy as jnp
from jax import lax
from jax.experimental import pallas as pl
from jax.experimental.pallas import tpu as pltpu
from jax.sharding import PartitionSpec as P

helm = 0.02
ITERS = 3
NF = 14
U, V, W, TH, G, CX, CY, CZ, A11, A22, A33, A12, A13, A23 = range(NF)
COMBOS = (
    (V, 6, TH, 2),
    (CY, 6, A12, 2),
    (U, 5, A22, 3),
    (W, 5, A11, 2),
    (G, 5, A33, 2),
    (CX, 5, A13, 2),
    (CZ, 5, A23, 2),
)
F32 = jnp.float32


def lanes(shape):
    return lax.broadcasted_iota(jnp.int32, shape, len(shape) - 1)


def rows(shape):
    return lax.broadcasted_iota(jnp.int32, shape, len(shape) - 2)


def roll(a, shift, axis):
    shift = shift % a.shape[axis]
    if shift == 0:
        return a
    return pltpu.roll(a, shift, axis)


def xs(a, d):
    return roll(a, -d, 1)


def ys(a, d):
    return roll(a, -d, 0)


def rim_x(q, d):
    c = lanes((48, 128)) % 8
    moved = roll(q, -d, 1)
    if d > 0:
        first = jnp.where(c == 7, roll(q[48:], 7, 1), moved[:48])
        return jnp.concatenate((first, moved[48:]), axis=0)
    last = jnp.where(c == 0, roll(q[:48], -7, 1), moved[48:])
    return jnp.concatenate((moved[:48], last), axis=0)


def rim_z(q, d):
    lane = lanes(q.shape)
    end = lane >= 120 if d > 0 else lane < 8
    return jnp.where(end, 0.0, roll(q, -8 * d, 1))


def rim_own(q):
    return jnp.where(lanes((8, 128)) % 8 < 4, q[56:64], q[32:40])


def upwind_weights(cx, cr, cy, cd, cz, cu, dens):
    ig = 1.0 / dens
    pos, neg = (lambda a: jnp.maximum(a, 0.0)), (lambda a: jnp.minimum(a, 0.0))
    rp, rn, lp, ln = pos(cr), neg(cr), pos(cx), neg(cx)
    dp, dn, up, un = pos(cd), neg(cd), pos(cy), neg(cy)
    ap, an, bp, bn = pos(cu), neg(cu), pos(cz), neg(cz)
    mid = 1.0 - ig * (((rp - ln) + (dp - un)) + (ap - bn))
    return mid, tuple(ig * a for a in (lp, -rn, up, -dn, bp, -an)), ig


def face(c, one, two):
    return 0.5 * (jnp.abs(c) - c * c / (0.5 * (one + two)))


def anti_weights(faces, ig):
    kl, kr, ku, kd, kb, ka = faces
    mid = 1.0 + ig * (((kl + kr) + (ku + kd)) + (ka + kb))
    return mid, tuple(-ig * a for a in faces)


def seven(mid, w, p, around):
    x = w[0] * around[0] + w[1] * around[1]
    y = w[2] * around[2] + w[3] * around[3]
    z = w[4] * around[4] + w[5] * around[5]
    return (mid * p + x) + (y + z)


def field_of(refs, f):
    mom, th, cou, den, dia, cro = refs
    if f < 3:
        return mom.at[f]
    if f == TH:
        return th
    if f == G:
        return den
    if f < 8:
        return cou.at[f - 5]
    if f < 11:
        return dia.at[f - 8]
    return cro.at[f - 11]


def strips(levels):
    nz = len(levels)
    slot = lanes(levels[0].shape) // 8
    left = right = jnp.zeros(levels[0].shape, F32)
    for k, a in enumerate(levels):
        moved = roll(a, 8 * k, 1)
        left = jnp.where(slot == k, moved, left)
        right = jnp.where(slot == (k - 1) % nz, moved, right)
    return left, roll(right, 8, 1)


def fetch_kernel(*refs):
    sources, refs, (to_chip, to_other, to_up, to_down, sem) = refs[:6], refs[6:12], refs[12:]
    copies = [pltpu.make_async_copy(a, b, sem.at[i]) for i, (a, b) in enumerate(zip(sources, refs))]
    for copy in copies:
        copy.start()
    for copy in copies:
        copy.wait()
    cou = refs[2]
    nz = refs[1].shape[0]
    row = rows((8, 128))
    first_row = (row == 0) & (lax.axis_index("gy") == 0)
    for k in range(nz):
        cou[1, k] = jnp.where(first_row, 0.0, cou[1, k])
    cou[2, 0] = jnp.zeros((8, 128), F32)
    for c, (first, n, second, m) in enumerate(COMBOS):
        one, two = field_of(refs, first), field_of(refs, second)
        for k in range(nz):
            a, b = one[k], two[k]
            to_down[c, k] = jnp.where(row < n, a, roll(b, n, 0))
            to_up[c, k] = jnp.where(row >= 8 - n, a, roll(b, -n, 0))
    for f in range(NF):
        ref = field_of(refs, f)
        left, right = strips([ref[k] for k in range(nz)])
        to_chip[f] = jnp.where(even_x(), right, left)
        to_other[f] = jnp.where(even_x(), left, right)


def even_x():
    return lax.axis_index("gx") % 2 == 0


def by_side(chip, other):
    return jnp.where(even_x(), other, chip), jnp.where(even_x(), chip, other)


def corner_tiles(strip):
    row = rows((8, 128))
    for c, (first, n, second, m) in enumerate(COMBOS):
        a, b = strip[first], strip[second]
        up = jnp.where(row >= 8 - n, a, roll(b, -n, 0))
        yield c, up, jnp.where(row < n, a, roll(b, n, 0))


def other_kernel(from_other, to_up, to_down):
    for c, up, down in corner_tiles(from_other):
        to_up[c] = up
        to_down[c] = down


def chip_kernel(from_chip, other_up, other_down, to_up, to_down):
    to_up[0] = other_up[...]
    to_down[0] = other_down[...]
    for c, up, down in corner_tiles(from_chip):
        to_up[1, c] = up
        to_down[1, c] = down


def halo(f, low, high):
    gy = lax.axis_index("gy")
    outside = 1.0 if f == G else 0.0
    return (
        jnp.where(gy > 0, low, outside),
        jnp.where(gy < lax.axis_size("gy") - 1, high, outside),
    )


def masks(shape):
    gy = lax.axis_index("gy")
    has_below = gy > 0
    has_above = gy < lax.axis_size("gy") - 1
    row = rows(shape) % 24
    inside = ((row >= 8) | has_below) & ((row < 16) | has_above)
    edge = ((row == 8) & ~has_below) | ((row == 16) & ~has_above)
    return inside, edge


def core_kernel(
    mom, th, cou, den, dia, cro, to_chip, to_other, below, above,
    moved, right_side, C, near_left, near_right, S, P1, M,
):
    refs = (mom, th, cou, den, dia, cro)
    nz = den.shape[0]
    shape = (24, 128)
    for c, (first, n, second, m) in enumerate(COMBOS):
        for f, shift in ((first, 0), (second, n)):
            ref = field_of(refs, f)
            outer = []
            for k in range(nz):
                low, high = halo(f, roll(below[c, k], shift, 0), roll(above[c, k], -shift, 0))
                S[f, k + 1] = jnp.concatenate((low, ref[k], high), axis=0)
                outer.append(jnp.concatenate((low, high), axis=0))
            own_strips = by_side(to_chip[f], to_other[f])
            for out, mid, ends in zip((near_left, near_right), own_strips, strips(outer)):
                out[f] = jnp.concatenate((ends[0:8], mid, ends[8:16]), axis=0)
            pad = jnp.full(shape, 1.0 if f == G else 0.0, F32)
            S[f, 0] = pad
            S[f, nz + 1] = pad
    inside, edge = masks(shape)
    zero = jnp.zeros(shape, F32)

    def upwind(k, carry):
        cx, cy, cz, cu = S[CX, k], S[CY, k], S[CZ, k], S[CZ, k + 1]
        mid, w, ig = upwind_weights(cx, xs(cx, 1), cy, ys(cy, 1), cz, cu, S[G, k])
        for f in range(4):
            psi = S[f, k]
            around = (xs(psi, -1), xs(psi, 1), ys(psi, -1), ys(psi, 1), S[f, k - 1], S[f, k + 1])
            P1[f, k] = seven(mid, w, psi, around)
        return carry

    lax.fori_loop(1, nz + 1, upwind, 0, unroll=8)
    for f in range(4):
        P1[f, 0] = zero
        P1[f, nz + 1] = zero

    def anti(k, kb):
        dens = S[G, k]
        kl = face(S[CX, k], xs(dens, -1), dens)
        ku = face(S[CY, k], ys(dens, -1), dens)
        ka = face(S[CZ, k + 1], dens, S[G, k + 1])
        mid, w = anti_weights((kl, xs(kl, 1), ku, ys(ku, 1), kb, ka), 1.0 / dens)
        for f in range(4):
            psi = P1[f, k]
            around = (xs(psi, -1), xs(psi, 1), ys(psi, -1), ys(psi, 1), P1[f, k - 1], P1[f, k + 1])
            res = seven(mid, w, psi, around)
            if f < 3:
                M[f, k] = res
            moved[f, k - 1] = res[8:16]
        return ka

    lax.fori_loop(1, nz + 1, anti, zero, unroll=8)
    M[2, 0] = zero
    M[2, nz + 1] = zero

    def first(k, carry):
        u, v = M[0, k], M[1, k]
        rhs = 0.5 * (
            (xs(u, 1) - xs(u, -1)) + (ys(v, 1) - ys(v, -1)) + (M[2, k + 1] - M[2, k - 1])
        )
        right_side[k - 1] = jnp.where(inside, rhs, 0.0)
        a11, a22, a33 = S[A11, k], S[A22, k], S[A33, k]
        wxl = 0.5 * (xs(a11, -1) + a11)
        wyl = jnp.where(edge, 0.0, 0.5 * (ys(a22, -1) + a22))
        wzl = jnp.where(k > 1, 0.5 * (S[A33, k - 1] + a33), 0.0)
        wz = jnp.where(k < nz, 0.5 * (S[A33, k + 1] + a33), 0.0)
        wx, wy = xs(wxl, 1), ys(wyl, 1)
        for n, w in enumerate((wx, wxl, wy, wyl, wz, wzl)):
            C[n, k - 1] = w
        C[6, k - 1] = ((wx + wxl) + (wy + wyl)) + ((wz + wzl) + helm)
        C[7, k - 1] = 0.25 * S[A12, k]
        C[8, k - 1] = 0.25 * S[A13, k]
        C[9, k - 1] = 0.25 * S[A23, k]
        return carry

    lax.fori_loop(1, nz + 1, first, 0, unroll=8)


def solve_kernel(
    right_side, C, near_left, near_right, from_chip, from_other, cbelow, cabove,
    basis, dxs, dys, rim_moved, rim_basis, rim_dxs, rim_dys, gram,
    VV, D, E, T,
):
    nz = right_side.shape[0]
    shape = (24, 128)
    zero = jnp.zeros(shape, F32)
    inside, edge = masks((96, 128))
    lane96 = lanes((96, 128))

    far = {}
    for c, (one, n, two, m) in enumerate(COMBOS):
        for f, shift in ((one, 0), (two, n)):
            far[f] = []
            lows = by_side(cbelow[1, c], cbelow[0, c])
            highs = by_side(cabove[1, c], cabove[0, c])
            for side, mine in enumerate(by_side(from_chip[f], from_other[f])):
                low, high = halo(f, roll(lows[side], shift, 0), roll(highs[side], -shift, 0))
                far[f].append(jnp.concatenate((low, mine, high), axis=0))

    def rim_field(f):
        return jnp.concatenate((far[f][0], near_right[f], near_left[f], far[f][1]), axis=0)

    def around(q):
        return (
            rim_x(q, -1), rim_x(q, 1), ys(q, -1), ys(q, 1), rim_z(q, -1), rim_z(q, 1)
        )

    cx, cy, cz, dens = rim_field(CX), rim_field(CY), rim_field(CZ), rim_field(G)
    cu = rim_z(cz, 1)
    mid, w, ig = upwind_weights(cx, rim_x(cx, 1), cy, ys(cy, 1), cz, cu, dens)
    kl = face(cx, rim_x(dens, -1), dens)
    ku = face(cy, ys(dens, -1), dens)
    kb = face(cz, roll(dens, 8, 1), dens)
    mid2, w2 = anti_weights((kl, rim_x(kl, 1), ku, ys(ku, 1), kb, rim_z(kb, 1)), ig)
    done = []
    for f in range(4):
        psi = rim_field(f)
        psi = seven(mid, w, psi, around(psi))
        psi = seven(mid2, w2, psi, around(psi))
        rim_moved[f] = rim_own(psi)
        done.append(psi)
    u, v, t = done[:3]
    v0 = 0.5 * (
        (rim_x(u, 1) - rim_x(u, -1)) + (ys(v, 1) - ys(v, -1)) + (rim_z(t, 1) - rim_z(t, -1))
    )
    v0 = jnp.where(inside, v0, 0.0)

    lane = lanes(shape)
    c24 = lane % 8
    slot = lane // 8
    edges = jnp.where(c24 < 4, v0[48:72], v0[24:48])
    turned = [roll(edges, -8 * k, 1) for k in range(nz)]
    inner = zero
    for k in range(nz):
        core = right_side[k]
        VV[0, k + 1] = jnp.where(
            lane < 4, turned[k], jnp.where(lane >= 124, turned[(k + 1) % nz], core)
        )
        take = ((slot == k) & (c24 >= 4)) | ((slot == (k - 1) % nz) & (c24 < 4))
        inner = jnp.where(take, roll(core, 8 * k, 1), inner)
    q = jnp.concatenate(
        (
            v0[0:24],
            jnp.where(c24 < 4, roll(inner, 8, 1), v0[24:48]),
            jnp.where(c24 >= 4, inner, v0[48:72]),
            v0[72:96],
        ),
        axis=0,
    )

    a11, a22, a33 = rim_field(A11), rim_field(A22), rim_field(A33)
    wxl = 0.5 * (rim_x(a11, -1) + a11)
    wyl = jnp.where(edge, 0.0, 0.5 * (ys(a22, -1) + a22))
    wzl = jnp.where(lane96 < 8, 0.0, 0.5 * (roll(a33, 8, 1) + a33))
    wx, wy, wz = rim_x(wxl, 1), ys(wyl, 1), rim_z(wzl, 1)
    wc = ((wx + wxl) + (wy + wyl)) + ((wz + wzl) + helm)
    q12, q13, q23 = (0.25 * rim_field(f) for f in (A12, A13, A23))
    rims = [rim_own(q)]
    rim_basis[0] = rims[0]
    for i in range(3):
        xm, xp, ym, yp, zm, zp = around(q)
        d, e = xp - xm, yp - ym
        rim_dxs[i] = rim_own(d)
        rim_dys[i] = rim_own(e)
        new = seven(-wc, (wxl, wx, wyl, wy, wzl, wz), q, (xm, xp, ym, yp, zm, zp))
        new = new + q12 * (ys(d, 1) - ys(d, -1))
        new = new + q13 * (rim_z(d, 1) - rim_z(d, -1))
        q = new + q23 * (rim_z(e, 1) - rim_z(e, -1))
        rims.append(rim_own(q))
        if i < 2:
            rim_basis[i + 1] = rims[-1]

    for i in range(3):
        VV[i, 0] = zero
        VV[i, nz + 1] = zero
    for a in (D, E):
        a[0] = zero
        a[nz + 1] = zero
    own = lambda a: a[8:16]
    sums = {}
    for i in range(3):
        last = i == 2
        cut = own if last else (lambda a: a)

        def flat(k, carry, i=i, cut=cut, last=last):
            p = VV[i, k]
            xp, xm, yp, ym = xs(p, 1), xs(p, -1), ys(p, 1), ys(p, -1)
            d, e = xp - xm, yp - ym
            D[k] = d
            E[k] = e
            dxs[i, k - 1] = own(d)
            dys[i, k - 1] = own(e)
            basis[i, k - 1] = own(p)
            near = (xp, xm, yp, ym, VV[i, k + 1], VV[i, k - 1])
            t = seven(-cut(C[6, k - 1]), [cut(C[n, k - 1]) for n in range(6)], cut(p), [cut(a) for a in near])
            t = t + cut(C[7, k - 1]) * cut(ys(d, 1) - ys(d, -1))
            if last:
                T[k, 8:16] = t
            else:
                T[k] = t
            return carry

        lax.fori_loop(1, nz + 1, flat, 0, unroll=8)
        pairs = [(j, i + 1) for j in range(i + 2)]

        def deep(k, acc, i=i, cut=cut, last=last, pairs=pairs):
            v = cut(T[k]) + cut(C[8, k - 1]) * (cut(D[k + 1]) - cut(D[k - 1]))
            v = v + cut(C[9, k - 1]) * (cut(E[k + 1]) - cut(E[k - 1]))
            if not last:
                VV[i + 1, k] = v
                v = own(v)
            vs = [own(VV[j, k]) for j in range(i + 1)] + [v]
            return tuple(s + vs[j] * v for s, (j, _) in zip(acc, pairs))

        start = (jnp.zeros((8, 128), F32),) * len(pairs)
        acc = lax.fori_loop(1, nz + 1, deep, start, unroll=8)
        for s, key in zip(acc, pairs):
            sums[key] = s
    lane8 = lanes((8, 128))
    core_part = (lane8 >= 4) & (lane8 < 124)
    line = lanes((1, 128))
    out = jnp.zeros((1, 128), F32)
    for n, (i, j) in enumerate(KEYS):
        s = jnp.where(core_part, sums[(i, j)], 0.0) + rims[i] * rims[j]
        s = jnp.sum(jnp.sum(s, axis=0, keepdims=True), axis=1, keepdims=True)
        out = jnp.where(line == n, s, out)
    gram[...] = jnp.broadcast_to(out, gram.shape)


KEYS = ((0, 1), (1, 1), (0, 2), (1, 2), (2, 2), (0, 3), (1, 3), (2, 3), (3, 3))


def weights(gram):
    def inner(a, b):
        total = 0.0
        for i in range(4):
            for j in range(4):
                if a[i] is not None and b[j] is not None:
                    total = total + a[i] * b[j] * gram[(min(i, j), max(i, j))]
        return total

    def less(a, s, b):
        out = []
        for one, two in zip(a, b):
            if two is None:
                out.append(one)
            else:
                out.append(-(s * two) if one is None else one - s * two)
        return out

    one = jnp.ones((1, 1), F32)
    r = [one, None, None, None]
    sol = [None] * 4
    dirs, images, norms = [r], [[None, one, None, None]], []
    for n in range(ITERS):
        norms.append(inner(images[n], images[n]))
        beta = inner(r, images[n]) / norms[n]
        sol = less(sol, -beta, dirs[n])
        r = less(r, beta, images[n])
        if n + 1 < ITERS:
            z = [None] + r[:3]
            new_dir, new_img = r, z
            for l in range(n + 1):
                alpha = inner(z, images[l]) / norms[l]
                new_dir = less(new_dir, alpha, dirs[l])
                new_img = less(new_img, alpha, images[l])
            dirs.append(new_dir)
            images.append(new_img)
    return sol[:3]


def last_kernel(
    partial, moved, basis, dxs, dys, rim_moved, rim_basis, rim_dxs, rim_dys,
    momenta_out, theta_out, pressure,
):
    nz = moved.shape[1]
    total = jnp.sum(partial[...], axis=0, keepdims=True)
    line = lanes(total.shape)
    gram = {
        key: jnp.sum(jnp.where(line == n, total, 0.0), axis=1, keepdims=True)
        for n, key in enumerate(KEYS)
    }
    c = [jnp.broadcast_to(s, (8, 128)) for s in weights(gram)]
    h = [0.5 * s for s in c]
    lane = lanes((8, 128))

    def mix(s, a):
        return (s[0] * a[0] + s[1] * a[1]) + s[2] * a[2]

    def joined(rim, core):
        turned = [roll(rim, -8 * k, 1) for k in range(nz)]
        return [
            jnp.where(lane < 4, turned[k], jnp.where(lane >= 124, turned[(k + 1) % nz], core[k]))
            for k in range(nz)
        ]

    p_rim = mix(c, rim_basis)
    p = joined(p_rim, [mix(c, [basis[i, k] for i in range(3)]) for k in range(nz)])
    for k in range(nz):
        pressure[k] = p[k]
    zero = jnp.zeros((8, 128), F32)
    for n, (diff, rim_diff) in enumerate(((dxs, rim_dxs), (dys, rim_dys))):
        core = [moved[n, k] - mix(h, [diff[i, k] for i in range(3)]) for k in range(nz)]
        for k, a in enumerate(joined(rim_moved[n] - mix(h, rim_diff), core)):
            momenta_out[n, k] = a
    for k, a in enumerate(joined(rim_moved[2], [moved[2, k] for k in range(nz)])):
        above = p[k + 1] if k + 1 < nz else zero
        below = p[k - 1] if k > 0 else zero
        momenta_out[2, k] = a - 0.5 * (above - below)
    for k, a in enumerate(joined(rim_moved[3], [moved[3, k] for k in range(nz)])):
        theta_out[k] = a


def shift_to(a, axis, step):
    n = lax.axis_size(axis)
    return lax.ppermute(a, axis, [(i, (i + step) % n) for i in range(n)])


def swap(a, axis, start):
    n = lax.axis_size(axis)
    pairs = []
    for i in range(start, n + start, 2):
        pairs += [(i % n, (i + 1) % n), ((i + 1) % n, i % n)]
    return lax.ppermute(a, axis, pairs)


def call(kernel, name, out, scratch=(), space=pltpu.VMEM, limit=16, cost=None):
    def run(*args):
        return pl.pallas_call(
            kernel,
            out_shape=tuple(jax.ShapeDtypeStruct(a, F32) for a in out),
            in_specs=[pl.BlockSpec(memory_space=space)] * len(args),
            out_specs=[pl.BlockSpec(memory_space=pltpu.VMEM)] * len(out),
            scratch_shapes=list(scratch),
            compiler_params=pltpu.CompilerParams(vmem_limit_bytes=limit << 20),
            cost_estimate=cost,
            name=name,
        )(*args)

    return run


def local(momenta, theta, courant, density, metric_diag, metric_cross):
    nz = density.shape[0]
    args = (momenta, theta, courant, density, metric_diag, metric_cross)
    block = (nz, 8, 128)
    core = (nz, 24, 128)
    deep = (nz + 2, 24, 128)
    nx, ny = lax.axis_size("gx"), lax.axis_size("gy")
    rows_out = (len(COMBOS), nz, 8, 128)

    tiles = (NF, 8, 128)
    *args, to_chip, to_other, to_up, to_down = call(
        fetch_kernel,
        "fetch",
        [a.shape for a in args] + [tiles] * 2 + [rows_out] * 2,
        [pltpu.SemaphoreType.DMA((6,))],
        pltpu.HBM,
    )(*(pltpu.with_memory_space_constraint(a, pltpu.HBM) for a in args))
    below = shift_to(to_up, "gy", 1)
    above = shift_to(to_down, "gy", -1)
    from_other = swap(to_other, "gx", 1)
    from_chip = swap(to_chip, "gx", 0)
    pair = (len(COMBOS), 8, 128)
    other_up, other_down = call(
        other_kernel,
        "other",
        [pair] * 2,
        cost=pl.CostEstimate(flops=10**10, transcendentals=0, bytes_accessed=10**9),
    )(from_other)
    corner_up, corner_down = call(chip_kernel, "chip", [(2,) + pair] * 2)(
        from_chip, other_up, other_down
    )
    cbelow = shift_to(corner_up, "gy", 1)
    cabove = shift_to(corner_down, "gy", -1)
    moved, right_side, coef, near_left, near_right = call(
        core_kernel,
        "core",
        [(4,) + block, core, (10,) + core] + [(NF, 24, 128)] * 2,
        [pltpu.VMEM((n,) + deep, F32) for n in (NF, 4, 3)],
    )(*args, to_chip, to_other, below, above)
    three, rim = (3,) + block, (3, 8, 128)
    *parts, gram = call(
        solve_kernel,
        "solve",
        [three] * 3 + [(4, 8, 128), rim, rim, rim, (nx, 128)],
        [pltpu.VMEM((3,) + deep, F32)] + [pltpu.VMEM(deep, F32)] * 3,
    )(right_side, coef, near_left, near_right, from_chip, from_other, cbelow, cabove)

    part = lax.all_to_all(gram, "gx", 0, 0, tiled=True)
    part = jnp.broadcast_to(jnp.sum(part, axis=0, keepdims=True), (ny, 128))
    part = lax.all_to_all(part, "gy", 0, 0, tiled=True)
    momenta_out, theta_out, pressure = call(
        last_kernel, "combine", [three, block, block]
    )(part, moved, *parts)
    return (momenta_out, theta_out, pressure)


def solution(mesh):
    placed = (
        P(None, None, "gy", "gx"),
        P(None, "gy", "gx"),
        P(None, None, "gy", "gx"),
        P(None, "gy", "gx"),
        P(None, None, "gy", "gx"),
        P(None, None, "gy", "gx"),
    )
    return jax.shard_map(
        local,
        mesh=mesh,
        in_specs=placed,
        out_specs=(P(None, None, "gy", "gx"), P(None, "gy", "gx"), P(None, "gy", "gx")),
        check_vma=False,
    )
```

```python
import jax
import jax.numpy as jnp
from jax import lax
from jax.experimental import pallas as pl
from jax.experimental.pallas import tpu as pltpu
from jax.sharding import PartitionSpec as P

helm = 0.02
ITERS = 3
NF = 14
U, V, W, TH, G, CX, CY, CZ, A11, A22, A33, A12, A13, A23 = range(NF)
COMBOS = (
    (V, 6, TH, 2),
    (CY, 6, A12, 2),
    (U, 5, A22, 3),
    (W, 5, A11, 2),
    (G, 5, A33, 2),
    (CX, 5, A13, 2),
    (CZ, 5, A23, 2),
)
F32 = jnp.float32


def lanes(shape):
    return lax.broadcasted_iota(jnp.int32, shape, len(shape) - 1)


def rows(shape):
    return lax.broadcasted_iota(jnp.int32, shape, len(shape) - 2)


def roll(a, shift, axis):
    shift = shift % a.shape[axis]
    if shift == 0:
        return a
    return pltpu.roll(a, shift, axis)


def xs(a, d):
    return roll(a, -d, 1)


def ys(a, d):
    return roll(a, -d, 0)


def rim_x(q, d):
    c = lanes((48, 128)) % 8
    moved = roll(q, -d, 1)
    if d > 0:
        first = jnp.where(c == 7, roll(q[48:], 7, 1), moved[:48])
        return jnp.concatenate((first, moved[48:]), axis=0)
    last = jnp.where(c == 0, roll(q[:48], -7, 1), moved[48:])
    return jnp.concatenate((moved[:48], last), axis=0)


def rim_z(q, d):
    lane = lanes(q.shape)
    end = lane >= 120 if d > 0 else lane < 8
    return jnp.where(end, 0.0, roll(q, -8 * d, 1))


def rim_own(q):
    return jnp.where(lanes((8, 128)) % 8 < 4, q[56:64], q[32:40])


def upwind_weights(cx, cr, cy, cd, cz, cu, dens):
    ig = 1.0 / dens
    pos, neg = (lambda a: jnp.maximum(a, 0.0)), (lambda a: jnp.minimum(a, 0.0))
    rp, rn, lp, ln = pos(cr), neg(cr), pos(cx), neg(cx)
    dp, dn, up, un = pos(cd), neg(cd), pos(cy), neg(cy)
    ap, an, bp, bn = pos(cu), neg(cu), pos(cz), neg(cz)
    mid = 1.0 - ig * (((rp - ln) + (dp - un)) + (ap - bn))
    return mid, tuple(ig * a for a in (lp, -rn, up, -dn, bp, -an)), ig


def face(c, one, two):
    return 0.5 * (jnp.abs(c) - c * c / (0.5 * (one + two)))


def anti_weights(faces, ig):
    kl, kr, ku, kd, kb, ka = faces
    mid = 1.0 + ig * (((kl + kr) + (ku + kd)) + (ka + kb))
    return mid, tuple(-ig * a for a in faces)


def seven(mid, w, p, around):
    x = w[0] * around[0] + w[1] * around[1]
    y = w[2] * around[2] + w[3] * around[3]
    z = w[4] * around[4] + w[5] * around[5]
    return (mid * p + x) + (y + z)


def field_of(refs, f):
    mom, th, cou, den, dia, cro = refs
    if f < 3:
        return mom.at[f]
    if f == TH:
        return th
    if f == G:
        return den
    if f < 8:
        return cou.at[f - 5]
    if f < 11:
        return dia.at[f - 8]
    return cro.at[f - 11]


def strips(levels):
    nz = len(levels)
    slot = lanes(levels[0].shape) // 8
    left = right = jnp.zeros(levels[0].shape, F32)
    for k, a in enumerate(levels):
        moved = roll(a, 8 * k, 1)
        left = jnp.where(slot == k, moved, left)
        right = jnp.where(slot == (k - 1) % nz, moved, right)
    return left, roll(right, 8, 1)


def fetch_kernel(*refs):
    sources, refs, (to_chip, to_other, to_up, to_down, sem) = refs[:6], refs[6:12], refs[12:]
    copies = [pltpu.make_async_copy(a, b, sem.at[i]) for i, (a, b) in enumerate(zip(sources, refs))]
    for copy in copies:
        copy.start()
    cou = refs[2]
    nz = refs[1].shape[0]
    row = rows((8, 128))
    first_row = (row == 0) & (lax.axis_index("gy") == 0)
    for i, fields in enumerate(((U, V, W), (TH,), (CX, CY, CZ), (G,), (A11, A22, A33), (A12, A13, A23))):
        copies[i].wait()
        if i == 2:
            for k in range(nz):
                cou[1, k] = jnp.where(first_row, 0.0, cou[1, k])
            cou[2, 0] = jnp.zeros((8, 128), F32)
        for f in fields:
            ref = field_of(refs, f)
            left, right = strips([ref[k] for k in range(nz)])
            to_chip[f] = jnp.where(even_x(), right, left)
            to_other[f] = jnp.where(even_x(), left, right)
    for c, (first, n, second, m) in enumerate(COMBOS):
        one, two = field_of(refs, first), field_of(refs, second)
        for k in range(nz):
            a, b = one[k], two[k]
            to_down[c, k] = jnp.where(row < n, a, roll(b, n, 0))
            to_up[c, k] = jnp.where(row >= 8 - n, a, roll(b, -n, 0))


def even_x():
    return lax.axis_index("gx") % 2 == 0


def by_side(chip, other):
    return jnp.where(even_x(), other, chip), jnp.where(even_x(), chip, other)


def corner_tiles(strip):
    row = rows((8, 128))
    for c, (first, n, second, m) in enumerate(COMBOS):
        a, b = strip[first], strip[second]
        up = jnp.where(row >= 8 - n, a, roll(b, -n, 0))
        yield c, up, jnp.where(row < n, a, roll(b, n, 0))


def other_kernel(from_other, to_up, to_down):
    for c, up, down in corner_tiles(from_other):
        to_up[c] = up
        to_down[c] = down


def chip_kernel(from_chip, other_up, other_down, to_up, to_down):
    to_up[0] = other_up[...]
    to_down[0] = other_down[...]
    for c, up, down in corner_tiles(from_chip):
        to_up[1, c] = up
        to_down[1, c] = down


def halo(f, low, high):
    gy = lax.axis_index("gy")
    outside = 1.0 if f == G else 0.0
    return (
        jnp.where(gy > 0, low, outside),
        jnp.where(gy < lax.axis_size("gy") - 1, high, outside),
    )


def masks(shape):
    gy = lax.axis_index("gy")
    has_below = gy > 0
    has_above = gy < lax.axis_size("gy") - 1
    row = rows(shape) % 24
    inside = ((row >= 8) | has_below) & ((row < 16) | has_above)
    edge = ((row == 8) & ~has_below) | ((row == 16) & ~has_above)
    return inside, edge


def core_kernel(
    mom, th, cou, den, dia, cro, to_chip, to_other, below, above,
    moved, right_side, C, near_left, near_right, S, P1, M,
):
    refs = (mom, th, cou, den, dia, cro)
    nz = den.shape[0]
    shape = (24, 128)
    for c, (first, n, second, m) in enumerate(COMBOS):
        for f, shift in ((first, 0), (second, n)):
            ref = field_of(refs, f)
            outer = []
            for k in range(nz):
                low, high = halo(f, roll(below[c, k], shift, 0), roll(above[c, k], -shift, 0))
                S[f, k + 1] = jnp.concatenate((low, ref[k], high), axis=0)
                outer.append(jnp.concatenate((low, high), axis=0))
            own_strips = by_side(to_chip[f], to_other[f])
            for out, mid, ends in zip((near_left, near_right), own_strips, strips(outer)):
                out[f] = jnp.concatenate((ends[0:8], mid, ends[8:16]), axis=0)
            pad = jnp.full(shape, 1.0 if f == G else 0.0, F32)
            S[f, 0] = pad
            S[f, nz + 1] = pad
    inside, edge = masks(shape)
    zero = jnp.zeros(shape, F32)

    def upwind(k, carry):
        cx, cy, cz, cu = S[CX, k], S[CY, k], S[CZ, k], S[CZ, k + 1]
        mid, w, ig = upwind_weights(cx, xs(cx, 1), cy, ys(cy, 1), cz, cu, S[G, k])
        for f in range(4):
            psi = S[f, k]
            around = (xs(psi, -1), xs(psi, 1), ys(psi, -1), ys(psi, 1), S[f, k - 1], S[f, k + 1])
            P1[f, k] = seven(mid, w, psi, around)
        return carry

    lax.fori_loop(1, nz + 1, upwind, 0, unroll=8)
    for f in range(4):
        P1[f, 0] = zero
        P1[f, nz + 1] = zero

    def anti(k, kb):
        dens = S[G, k]
        kl = face(S[CX, k], xs(dens, -1), dens)
        ku = face(S[CY, k], ys(dens, -1), dens)
        ka = face(S[CZ, k + 1], dens, S[G, k + 1])
        mid, w = anti_weights((kl, xs(kl, 1), ku, ys(ku, 1), kb, ka), 1.0 / dens)
        for f in range(4):
            psi = P1[f, k]
            around = (xs(psi, -1), xs(psi, 1), ys(psi, -1), ys(psi, 1), P1[f, k - 1], P1[f, k + 1])
            res = seven(mid, w, psi, around)
            if f < 3:
                M[f, k] = res
            moved[f, k - 1] = res[8:16]
        return ka

    lax.fori_loop(1, nz + 1, anti, zero, unroll=8)
    M[2, 0] = zero
    M[2, nz + 1] = zero

    def first(k, carry):
        u, v = M[0, k], M[1, k]
        rhs = 0.5 * (
            (xs(u, 1) - xs(u, -1)) + (ys(v, 1) - ys(v, -1)) + (M[2, k + 1] - M[2, k - 1])
        )
        right_side[k - 1] = jnp.where(inside, rhs, 0.0)
        a11, a22, a33 = S[A11, k], S[A22, k], S[A33, k]
        wxl = 0.5 * (xs(a11, -1) + a11)
        wyl = jnp.where(edge, 0.0, 0.5 * (ys(a22, -1) + a22))
        wzl = jnp.where(k > 1, 0.5 * (S[A33, k - 1] + a33), 0.0)
        wz = jnp.where(k < nz, 0.5 * (S[A33, k + 1] + a33), 0.0)
        wx, wy = xs(wxl, 1), ys(wyl, 1)
        for n, w in enumerate((wx, wxl, wy, wyl, wz, wzl)):
            C[n, k - 1] = w
        C[6, k - 1] = ((wx + wxl) + (wy + wyl)) + ((wz + wzl) + helm)
        C[7, k - 1] = 0.25 * S[A12, k]
        C[8, k - 1] = 0.25 * S[A13, k]
        C[9, k - 1] = 0.25 * S[A23, k]
        return carry

    lax.fori_loop(1, nz + 1, first, 0, unroll=8)


def solve_kernel(
    right_side, C, near_left, near_right, from_chip, from_other, cbelow, cabove,
    basis, dxs, dys, rim_moved, rim_basis, rim_dxs, rim_dys, gram,
    VV, D, E, T,
):
    nz = right_side.shape[0]
    shape = (24, 128)
    zero = jnp.zeros(shape, F32)
    inside, edge = masks((96, 128))
    lane96 = lanes((96, 128))

    far = {}
    for c, (one, n, two, m) in enumerate(COMBOS):
        for f, shift in ((one, 0), (two, n)):
            far[f] = []
            lows = by_side(cbelow[1, c], cbelow[0, c])
            highs = by_side(cabove[1, c], cabove[0, c])
            for side, mine in enumerate(by_side(from_chip[f], from_other[f])):
                low, high = halo(f, roll(lows[side], shift, 0), roll(highs[side], -shift, 0))
                far[f].append(jnp.concatenate((low, mine, high), axis=0))

    def rim_field(f):
        return jnp.concatenate((far[f][0], near_right[f], near_left[f], far[f][1]), axis=0)

    def around(q):
        return (
            rim_x(q, -1), rim_x(q, 1), ys(q, -1), ys(q, 1), rim_z(q, -1), rim_z(q, 1)
        )

    cx, cy, cz, dens = rim_field(CX), rim_field(CY), rim_field(CZ), rim_field(G)
    cu = rim_z(cz, 1)
    mid, w, ig = upwind_weights(cx, rim_x(cx, 1), cy, ys(cy, 1), cz, cu, dens)
    kl = face(cx, rim_x(dens, -1), dens)
    ku = face(cy, ys(dens, -1), dens)
    kb = face(cz, roll(dens, 8, 1), dens)
    mid2, w2 = anti_weights((kl, rim_x(kl, 1), ku, ys(ku, 1), kb, rim_z(kb, 1)), ig)
    done = []
    for f in range(4):
        psi = rim_field(f)
        psi = seven(mid, w, psi, around(psi))
        psi = seven(mid2, w2, psi, around(psi))
        rim_moved[f] = rim_own(psi)
        done.append(psi)
    u, v, t = done[:3]
    v0 = 0.5 * (
        (rim_x(u, 1) - rim_x(u, -1)) + (ys(v, 1) - ys(v, -1)) + (rim_z(t, 1) - rim_z(t, -1))
    )
    v0 = jnp.where(inside, v0, 0.0)

    lane = lanes(shape)
    c24 = lane % 8
    slot = lane // 8
    edges = jnp.where(c24 < 4, v0[48:72], v0[24:48])
    turned = [roll(edges, -8 * k, 1) for k in range(nz)]
    inner = zero
    for k in range(nz):
        core = right_side[k]
        VV[0, k + 1] = jnp.where(
            lane < 4, turned[k], jnp.where(lane >= 124, turned[(k + 1) % nz], core)
        )
        take = ((slot == k) & (c24 >= 4)) | ((slot == (k - 1) % nz) & (c24 < 4))
        inner = jnp.where(take, roll(core, 8 * k, 1), inner)
    q = jnp.concatenate(
        (
            v0[0:24],
            jnp.where(c24 < 4, roll(inner, 8, 1), v0[24:48]),
            jnp.where(c24 >= 4, inner, v0[48:72]),
            v0[72:96],
        ),
        axis=0,
    )

    a11, a22, a33 = rim_field(A11), rim_field(A22), rim_field(A33)
    wxl = 0.5 * (rim_x(a11, -1) + a11)
    wyl = jnp.where(edge, 0.0, 0.5 * (ys(a22, -1) + a22))
    wzl = jnp.where(lane96 < 8, 0.0, 0.5 * (roll(a33, 8, 1) + a33))
    wx, wy, wz = rim_x(wxl, 1), ys(wyl, 1), rim_z(wzl, 1)
    wc = ((wx + wxl) + (wy + wyl)) + ((wz + wzl) + helm)
    q12, q13, q23 = (0.25 * rim_field(f) for f in (A12, A13, A23))
    rims = [rim_own(q)]
    rim_basis[0] = rims[0]
    for i in range(3):
        xm, xp, ym, yp, zm, zp = around(q)
        d, e = xp - xm, yp - ym
        rim_dxs[i] = rim_own(d)
        rim_dys[i] = rim_own(e)
        new = seven(-wc, (wxl, wx, wyl, wy, wzl, wz), q, (xm, xp, ym, yp, zm, zp))
        new = new + q12 * (ys(d, 1) - ys(d, -1))
        new = new + q13 * (rim_z(d, 1) - rim_z(d, -1))
        q = new + q23 * (rim_z(e, 1) - rim_z(e, -1))
        rims.append(rim_own(q))
        if i < 2:
            rim_basis[i + 1] = rims[-1]

    for i in range(3):
        VV[i, 0] = zero
        VV[i, nz + 1] = zero
    for a in (D, E):
        a[0] = zero
        a[nz + 1] = zero
    own = lambda a: a[8:16]
    sums = {}
    for i in range(3):
        last = i == 2
        cut = own if last else (lambda a: a)

        def flat(k, carry, i=i, cut=cut, last=last):
            p = VV[i, k]
            xp, xm, yp, ym = xs(p, 1), xs(p, -1), ys(p, 1), ys(p, -1)
            d, e = xp - xm, yp - ym
            D[k] = d
            E[k] = e
            dxs[i, k - 1] = own(d)
            dys[i, k - 1] = own(e)
            basis[i, k - 1] = own(p)
            near = (xp, xm, yp, ym, VV[i, k + 1], VV[i, k - 1])
            t = seven(-cut(C[6, k - 1]), [cut(C[n, k - 1]) for n in range(6)], cut(p), [cut(a) for a in near])
            t = t + cut(C[7, k - 1]) * cut(ys(d, 1) - ys(d, -1))
            if last:
                T[k, 8:16] = t
            else:
                T[k] = t
            return carry

        lax.fori_loop(1, nz + 1, flat, 0, unroll=8)
        pairs = [(j, i + 1) for j in range(i + 2)]

        def deep(k, acc, i=i, cut=cut, last=last, pairs=pairs):
            v = cut(T[k]) + cut(C[8, k - 1]) * (cut(D[k + 1]) - cut(D[k - 1]))
            v = v + cut(C[9, k - 1]) * (cut(E[k + 1]) - cut(E[k - 1]))
            if not last:
                VV[i + 1, k] = v
                v = own(v)
            vs = [own(VV[j, k]) for j in range(i + 1)] + [v]
            return tuple(s + vs[j] * v for s, (j, _) in zip(acc, pairs))

        start = (jnp.zeros((8, 128), F32),) * len(pairs)
        acc = lax.fori_loop(1, nz + 1, deep, start, unroll=8)
        for s, key in zip(acc, pairs):
            sums[key] = s
    lane8 = lanes((8, 128))
    core_part = (lane8 >= 4) & (lane8 < 124)
    line = lanes((1, 128))
    out = jnp.zeros((1, 128), F32)
    for n, (i, j) in enumerate(KEYS):
        s = jnp.where(core_part, sums[(i, j)], 0.0) + rims[i] * rims[j]
        s = jnp.sum(jnp.sum(s, axis=0, keepdims=True), axis=1, keepdims=True)
        out = jnp.where(line == n, s, out)
    gram[...] = jnp.broadcast_to(out, gram.shape)


KEYS = ((0, 1), (1, 1), (0, 2), (1, 2), (2, 2), (0, 3), (1, 3), (2, 3), (3, 3))


def weights(gram):
    def inner(a, b):
        total = 0.0
        for i in range(4):
            for j in range(4):
                if a[i] is not None and b[j] is not None:
                    total = total + a[i] * b[j] * gram[(min(i, j), max(i, j))]
        return total

    def less(a, s, b):
        out = []
        for one, two in zip(a, b):
            if two is None:
                out.append(one)
            else:
                out.append(-(s * two) if one is None else one - s * two)
        return out

    one = jnp.ones((1, 1), F32)
    r = [one, None, None, None]
    sol = [None] * 4
    dirs, images, norms = [r], [[None, one, None, None]], []
    for n in range(ITERS):
        norms.append(inner(images[n], images[n]))
        beta = inner(r, images[n]) / norms[n]
        sol = less(sol, -beta, dirs[n])
        r = less(r, beta, images[n])
        if n + 1 < ITERS:
            z = [None] + r[:3]
            new_dir, new_img = r, z
            for l in range(n + 1):
                alpha = inner(z, images[l]) / norms[l]
                new_dir = less(new_dir, alpha, dirs[l])
                new_img = less(new_img, alpha, images[l])
            dirs.append(new_dir)
            images.append(new_img)
    return sol[:3]


def last_kernel(
    partial, moved, basis, dxs, dys, rim_moved, rim_basis, rim_dxs, rim_dys,
    momenta_out, theta_out, pressure,
):
    nz = moved.shape[1]
    total = jnp.sum(partial[...], axis=0, keepdims=True)
    line = lanes(total.shape)
    gram = {
        key: jnp.sum(jnp.where(line == n, total, 0.0), axis=1, keepdims=True)
        for n, key in enumerate(KEYS)
    }
    c = [jnp.broadcast_to(s, (8, 128)) for s in weights(gram)]
    h = [0.5 * s for s in c]
    lane = lanes((8, 128))

    def mix(s, a):
        return (s[0] * a[0] + s[1] * a[1]) + s[2] * a[2]

    def joined(rim, core):
        turned = [roll(rim, -8 * k, 1) for k in range(nz)]
        return [
            jnp.where(lane < 4, turned[k], jnp.where(lane >= 124, turned[(k + 1) % nz], core[k]))
            for k in range(nz)
        ]

    p_rim = mix(c, rim_basis)
    p = joined(p_rim, [mix(c, [basis[i, k] for i in range(3)]) for k in range(nz)])
    for k in range(nz):
        pressure[k] = p[k]
    zero = jnp.zeros((8, 128), F32)
    for n, (diff, rim_diff) in enumerate(((dxs, rim_dxs), (dys, rim_dys))):
        core = [moved[n, k] - mix(h, [diff[i, k] for i in range(3)]) for k in range(nz)]
        for k, a in enumerate(joined(rim_moved[n] - mix(h, rim_diff), core)):
            momenta_out[n, k] = a
    for k, a in enumerate(joined(rim_moved[2], [moved[2, k] for k in range(nz)])):
        above = p[k + 1] if k + 1 < nz else zero
        below = p[k - 1] if k > 0 else zero
        momenta_out[2, k] = a - 0.5 * (above - below)
    for k, a in enumerate(joined(rim_moved[3], [moved[3, k] for k in range(nz)])):
        theta_out[k] = a


def shift_to(a, axis, step):
    n = lax.axis_size(axis)
    return lax.ppermute(a, axis, [(i, (i + step) % n) for i in range(n)])


def swap(a, axis, start):
    n = lax.axis_size(axis)
    pairs = []
    for i in range(start, n + start, 2):
        pairs += [(i % n, (i + 1) % n), ((i + 1) % n, i % n)]
    return lax.ppermute(a, axis, pairs)


def call(kernel, name, out, scratch=(), space=pltpu.VMEM, limit=16, cost=None):
    def run(*args):
        return pl.pallas_call(
            kernel,
            out_shape=tuple(jax.ShapeDtypeStruct(a, F32) for a in out),
            in_specs=[pl.BlockSpec(memory_space=space)] * len(args),
            out_specs=[pl.BlockSpec(memory_space=pltpu.VMEM)] * len(out),
            scratch_shapes=list(scratch),
            compiler_params=pltpu.CompilerParams(vmem_limit_bytes=limit << 20),
            cost_estimate=cost,
            name=name,
        )(*args)

    return run


def local(momenta, theta, courant, density, metric_diag, metric_cross):
    nz = density.shape[0]
    args = (momenta, theta, courant, density, metric_diag, metric_cross)
    block = (nz, 8, 128)
    core = (nz, 24, 128)
    deep = (nz + 2, 24, 128)
    nx, ny = lax.axis_size("gx"), lax.axis_size("gy")
    rows_out = (len(COMBOS), nz, 8, 128)

    tiles = (NF, 8, 128)
    *args, to_chip, to_other, to_up, to_down = call(
        fetch_kernel,
        "fetch",
        [a.shape for a in args] + [tiles] * 2 + [rows_out] * 2,
        [pltpu.SemaphoreType.DMA((6,))],
        pltpu.HBM,
    )(*(pltpu.with_memory_space_constraint(a, pltpu.HBM) for a in args))
    below = shift_to(to_up, "gy", 1)
    above = shift_to(to_down, "gy", -1)
    from_other = swap(to_other, "gx", 1)
    from_chip = swap(to_chip, "gx", 0)
    pair = (len(COMBOS), 8, 128)
    other_up, other_down = call(
        other_kernel,
        "other",
        [pair] * 2,
        cost=pl.CostEstimate(flops=10**10, transcendentals=0, bytes_accessed=10**9),
    )(from_other)
    corner_up, corner_down = call(chip_kernel, "chip", [(2,) + pair] * 2)(
        from_chip, other_up, other_down
    )
    cbelow = shift_to(corner_up, "gy", 1)
    cabove = shift_to(corner_down, "gy", -1)
    moved, right_side, coef, near_left, near_right = call(
        core_kernel,
        "core",
        [(4,) + block, core, (10,) + core] + [(NF, 24, 128)] * 2,
        [pltpu.VMEM((n,) + deep, F32) for n in (NF, 4, 3)],
    )(*args, to_chip, to_other, below, above)
    three, rim = (3,) + block, (3, 8, 128)
    *parts, gram = call(
        solve_kernel,
        "solve",
        [three] * 3 + [(4, 8, 128), rim, rim, rim, (nx, 128)],
        [pltpu.VMEM((3,) + deep, F32)] + [pltpu.VMEM(deep, F32)] * 3,
    )(right_side, coef, near_left, near_right, from_chip, from_other, cbelow, cabove)

    part = lax.all_to_all(gram, "gx", 0, 0, tiled=True)
    part = jnp.broadcast_to(jnp.sum(part, axis=0, keepdims=True), (ny, 128))
    part = lax.all_to_all(part, "gy", 0, 0, tiled=True)
    momenta_out, theta_out, pressure = call(
        last_kernel, "combine", [three, block, block]
    )(part, moved, *parts)
    return (momenta_out, theta_out, pressure)


def solution(mesh):
    placed = (
        P(None, None, "gy", "gx"),
        P(None, "gy", "gx"),
        P(None, None, "gy", "gx"),
        P(None, "gy", "gx"),
        P(None, None, "gy", "gx"),
        P(None, None, "gy", "gx"),
    )
    return jax.shard_map(
        local,
        mesh=mesh,
        in_specs=placed,
        out_specs=(P(None, None, "gy", "gx"), P(None, "gy", "gx"), P(None, "gy", "gx")),
        check_vma=False,
    )
```
